256 devices in a mesh: dom: 32 (over z, x), rep: 8 (over y, core).
Axes of the slice: x: 4, y: 4, z: 8, core: 2. Of those that a mesh axis runs over, the one named last changes fastest.
Arguments:
- grad_out: bfloat16 [262144, 512], P(('dom', 'rep')), may hold values from -6 to 6
- features: bfloat16 [262144, 512], P(('dom', 'rep')), may hold values from -24 to 24
- weight: bfloat16 [512, 512], replicated, may hold values from -0.25 to 0.25
- edge_blocks: bfloat16 [32768, 128, 128], P(('dom', 'rep')), may hold values from -0.25 to 0.25
- block_index: int32 [32768, 2], P(('dom', 'rep')), may hold values from 0 to 63, as said below
- block_count: int32 [256], P(('dom', 'rep')), may hold values from 25 to 128, as said below
- node_perm: int32 [262144], P(('dom', 'rep')), may hold values from 0 to 262143, as said below
Outputs:
- grad_input: bfloat16 [262144, 512], P(('dom', 'rep'))
- weight_grad: float32 [512, 512], P('dom', 'rep')
The draws below stay inside these ranges and needn't reach their ends.
Inputs may be any that keep to these rules, and one draw needn't show every extreme that they name: A node at input row i, held by device s = i // 1024, lands at node_perm[i] = t * 1024 + s * 4 + k with 0 <= k < 4; each device's rows cover every pair (t, k) exactly once, so every device passes exactly 4 rows to every device. `block_index`: first column below 64, second below 8; blocks may repeat. `block_count`: in each group of 8 devices along rep exactly one device has 128 live slots; the others have between 25 and 64.
All inputs are finite; a program needn't handle non-finite values.
Results may differ from the reference program's by a relative error of at most 0.005.
Values may be sent and summed in bfloat16 or wider, within the bound.
A program may use at most 64 MiB of HBM per device.

```python
import math
import jax
import jax.numpy as jnp
from jax import lax

FIN = 512
FOUT = 512
BS = 128
ROWS_DEV = 1024
NB_DEV = 128
NODES = 262144
SLOT_ROWS = 4
PB = 64
CB = 8
NB_ALL = 32768
N_DOM = 32
N_REP = 8


def draw_node_perm(key, part):

    def one_device(device_index):
        local_keys = jax.random.permutation(jax.random.fold_in(key, device_index), ROWS_DEV)
        target_device = local_keys // SLOT_ROWS
        within_slot = local_keys % SLOT_ROWS
        return target_device * ROWS_DEV + device_index * SLOT_ROWS + within_slot
    return jax.vmap(one_device)(jnp.arange(N_DOM * N_REP)).reshape(NODES).astype(jnp.int32)


def draw_block_index(key, part):
    row_key = jax.random.fold_in(key, 11)
    col_key = jax.random.fold_in(key, 23)
    block_rows = jax.random.randint(row_key, (NB_ALL, 1), 0, PB)
    block_cols = jax.random.randint(col_key, (NB_ALL, 1), 0, CB)
    return jnp.concatenate([block_rows, block_cols], axis=1).astype(jnp.int32)


def draw_block_count(key, part):
    busy_key = jax.random.fold_in(key, 5)
    light_key = jax.random.fold_in(key, 7)
    busiest = jax.random.randint(busy_key, (N_DOM,), 0, N_REP)
    lighter = jax.random.randint(light_key, (N_DOM, N_REP), NB_DEV // 5, NB_DEV // 2 + 1)
    filled = jnp.where(jnp.arange(N_REP)[None, :] == busiest[:, None], NB_DEV, lighter)
    return filled.reshape(N_DOM * N_REP).astype(jnp.int32)


def raised(array, key, source, target, shards_of, factor):
    owner, partner = [(jnp.arange(array.shape[position]) // (array.shape[position] // shards_of)).reshape([-1 if axis == position else 1 for axis in range(array.ndim)]) for position in (source, target)]
    chosen = jax.random.permutation(key, shards_of)[partner]
    strong = (owner == chosen) | (owner == (partner + shards_of // 2) % shards_of)
    return jnp.where(strong, factor * array, array)


def block_levels(own_key, shape, split, least, top_value):
    def one(position, blocks):
        steps = jax.random.uniform(jax.random.fold_in(jax.random.fold_in(own_key, 6), position), (blocks,), jnp.float32, least / len(split), top_value / len(split))
        return jnp.repeat(jnp.exp(steps), shape[position] // blocks).reshape((-1,) + (1,) * (len(shape) - position - 1))

    factor_of = one(*split[0])
    for cut in split[1:]:
        factor_of = factor_of * one(*cut)
    return factor_of


def noise(rng, dims, width, limit, cuts=(), kind=jnp.bfloat16):
    values = width * jax.random.normal(rng, dims, jnp.float32)
    if cuts:
        values = values * block_levels(rng, dims, cuts, -0.22, 0.18)
    return jnp.clip(values, -limit, limit).astype(kind)


def gaussian_with(key, dims, deviation, limit, shards, heavy, dtype=jnp.bfloat16):
    entries = deviation * jax.random.normal(key, dims, jnp.float32)
    if shards:
        entries = entries * block_levels(key, dims, shards, -0.22, 0.18)
    return jnp.clip(raised(entries, jax.random.fold_in(key, 3), *heavy), -limit, limit).astype(dtype)


def setup_inputs(seed: int = 0) -> dict:
    key_list = jax.random.split(jax.random.key(seed), 8)
    return {
        "grad_out": noise(key_list[0], (NODES, FOUT), 1.0, 6.0, ((0, 256),)),
        "features": gaussian_with(key_list[1], (NODES, FIN), 1.0, 24.0, ((0, 256),), (0, 1, 256, 6.0)),
        "weight": noise(key_list[2], (FIN, FOUT), FIN ** -0.5, 0.25),
        "edge_blocks": noise(key_list[3], (NB_ALL, BS, BS), (4 * BS) ** -0.5, 0.25, ((0, 256),)),
        "block_index": draw_block_index(jax.random.fold_in(key_list[7], 71), 0),
        "block_count": draw_block_count(jax.random.fold_in(key_list[7], 71), 0),
        "node_perm": draw_node_perm(jax.random.fold_in(key_list[7], 71), 0),
    }


def reference(grad_out, features, weight, edge_blocks, block_index, block_count, node_perm):
    regrouped = jnp.zeros_like(grad_out).at[node_perm].set(grad_out)
    part_rows = regrouped.reshape(N_DOM, PB, BS, FOUT)
    blocks_dev = edge_blocks.reshape(N_DOM * N_REP, NB_DEV, BS, BS)
    index_dev = block_index.reshape(N_DOM * N_REP, NB_DEV, 2)

    def one_device(device_args):
        device_index, block_part, index_part, live_count = device_args
        partition = device_index // N_REP
        source = jnp.take(part_rows[partition], index_part[:, 0], axis=0)
        alive_mask = (jnp.arange(NB_DEV) < live_count).astype(jnp.float32)
        products = jnp.einsum('kij,kif->kjf', block_part.astype(jnp.float32), source.astype(jnp.float32))
        onehot = (index_part[:, 1][:, None] == jnp.arange(CB)[None, :]).astype(jnp.float32) * alive_mask[:, None]
        summed = jnp.einsum('kc,kjf->cjf', onehot, products, precision=lax.Precision.HIGHEST)
        return summed.astype(jnp.bfloat16)
    aggregated = lax.map(one_device, (jnp.arange(N_DOM * N_REP).astype(jnp.int32), blocks_dev, index_dev, block_count))
    aggregated = aggregated.reshape(NODES, FOUT)
    grad_input = jnp.dot(aggregated, weight.T, preferred_element_type=jnp.float32).astype(jnp.bfloat16)
    weight_grad = jnp.dot(features.T, aggregated, preferred_element_type=jnp.float32) * (1.0 / math.sqrt(NODES))
    return (grad_input, weight_grad)
```

```python
import math

import jax
import jax.numpy as jnp
from jax import lax
from jax.experimental import pallas as pl
from jax.experimental.pallas import tpu as pltpu
from jax.sharding import PartitionSpec as P


def cut_along(x, dim, length):
    before, after = (x.shape[:dim], x.shape[dim + 1 :])
    return jnp.moveaxis(x.reshape(*before, length, -1, *after), dim, 0)


def in_order(parts, dim):
    parts = jnp.moveaxis(parts, 0, dim)
    shape = parts.shape
    return parts.reshape(*shape[:dim], shape[dim] * shape[dim + 1], *shape[dim + 2 :])


def one_exchange(x, axis, axes, splits, concats):
    sizes = [lax.axis_size(a) for a in axes]
    parts = cut_along(x, splits[0], sizes[0])
    parts = jnp.moveaxis(cut_along(parts, splits[1] + 1, sizes[1]), 0, 1)
    inside = parts.shape[2:]
    parts = parts.reshape(-1, *inside)
    parts = lax.all_to_all(parts, axis, split_axis=0, concat_axis=0, tiled=True)
    parts = in_order(parts.reshape(*sizes, *inside), concats[0] + 1)
    return in_order(parts, concats[1])


def sent_and_summed(x, axis, dim):
    parts = cut_along(x, dim, lax.axis_size(axis))
    arrived = lax.all_to_all(parts, axis, split_axis=0, concat_axis=0, tiled=True)
    return arrived.sum(axis=0)


def slots_kernel(scale, index_ref, count_ref, src_ref, edge_ref, feat_ref, weight_ref,
                 gi_ref, wg_ref, acc_ref):
    acc_ref[...] = jnp.zeros_like(acc_ref)

    @pl.loop(0, count_ref[0])
    def _(s):
        b = index_ref[2 * s]
        c = index_ref[2 * s + 1]
        acc_ref[c] += lax.dot_general(
            edge_ref[s], src_ref[b], (((0,), (0,)), ((), ())),
            preferred_element_type=jnp.float32)

    side = acc_ref.shape[1]

    @pl.loop(0, acc_ref.shape[0])
    def _(c):
        rows = pl.ds(pl.multiple_of(c * side, side), side)
        agg = acc_ref[c].astype(jnp.bfloat16)
        gi_ref[rows, :] = lax.dot_general(
            agg, weight_ref[...], (((1,), (1,)), ((), ())),
            preferred_element_type=jnp.float32).astype(gi_ref.dtype)
        part = lax.dot_general(
            feat_ref[rows, :], agg, (((0,), (0,)), ((), ())),
            preferred_element_type=jnp.float32)

        @pl.when(c == 0)
        def _():
            wg_ref[...] = part

        @pl.when(c > 0)
        def _():
            wg_ref[...] += part

    wg_ref[...] = wg_ref[...] * scale


def slots(scale, index, count, src, edge, feat, weight):
    rows, width = feat.shape
    side = edge.shape[1]
    smem = pl.BlockSpec(memory_space=pltpu.SMEM)
    vmem = pl.BlockSpec(memory_space=pltpu.VMEM)
    return pl.pallas_call(
        lambda *refs: slots_kernel(scale, *refs),
        out_shape=(jax.ShapeDtypeStruct((rows, weight.shape[0]), jnp.bfloat16),
                   jax.ShapeDtypeStruct((width, src.shape[2]), jnp.float32)),
        in_specs=[smem, smem, vmem, vmem, vmem, vmem],
        out_specs=(vmem, vmem),
        scratch_shapes=[pltpu.VMEM((rows // side, side, src.shape[2]), jnp.float32)],
        compiler_params=pltpu.CompilerParams(vmem_limit_bytes=40 << 20),
        name="slots",
    )(index.reshape(-1), count, src, edge, feat, weight)


def on_device(grad_out, features, weight, edge_blocks, block_index, block_count, node_perm):
    dom_count = lax.axis_size("dom")
    rep_count = lax.axis_size("rep")
    device_count = dom_count * rep_count
    row_count = grad_out.shape[0]
    feat_width = grad_out.shape[1]
    slot_rows = row_count // device_count
    block_side = edge_blocks.shape[1]
    target_device = node_perm // row_count
    within_slot = node_perm % slot_rows
    target_slot = target_device * slot_rows + within_slot
    onehot = (jnp.arange(row_count)[:, None] == target_slot[None, :]).astype(jnp.bfloat16)
    ordered = jnp.dot(onehot, grad_out, preferred_element_type=jnp.float32).astype(jnp.bfloat16)
    ordered = ordered.reshape(dom_count, rep_count, slot_rows, feat_width)
    arrived = one_exchange(ordered, ("dom", "rep"), ("dom", "rep"), (0, 1), (0, 1))
    local_rows = arrived.reshape(row_count, feat_width)
    whole = lax.all_gather(local_rows, "rep", axis=0, tiled=True)
    stacked = whole.reshape(-1, block_side, feat_width)
    scale_factor = 1.0 / math.sqrt(row_count * device_count)
    grad_input, partial = slots(
        scale_factor, block_index, block_count, stacked, edge_blocks, features, weight)
    partial_cols = sent_and_summed(partial, "rep", 1)
    weight_grad = sent_and_summed(partial_cols, "dom", 0)
    return (grad_input, weight_grad)


def solution(mesh):
    in_specs = (
        P(("dom", "rep"), None),
        P(("dom", "rep"), None),
        P(),
        P(("dom", "rep"), None, None),
        P(("dom", "rep"), None),
        P(("dom", "rep")),
        P(("dom", "rep")),
    )
    out_specs = (P(("dom", "rep"), None), P("dom", "rep"))
    return jax.shard_map(
        on_device, mesh=mesh, in_specs=in_specs, out_specs=out_specs, check_vma=False
    )
```

```python
import math

import jax
import jax.numpy as jnp
from jax import lax
from jax.experimental import pallas as pl
from jax.experimental.pallas import tpu as pltpu
from jax.sharding import PartitionSpec as P


def slots_kernel(scale, index_ref, count_ref, src_ref, edge_ref, feat_ref, weight_ref,
                 gi_ref, wg_ref, acc_ref):
    acc_ref[...] = jnp.zeros_like(acc_ref)

    @pl.loop(0, count_ref[0])
    def _(s):
        b = index_ref[2 * s]
        c = index_ref[2 * s + 1]
        acc_ref[c] += lax.dot_general(
            edge_ref[s], src_ref[b], (((0,), (0,)), ((), ())),
            preferred_element_type=jnp.float32)

    side = acc_ref.shape[1]

    @pl.loop(0, acc_ref.shape[0])
    def _(c):
        rows = pl.ds(pl.multiple_of(c * side, side), side)
        agg = acc_ref[c].astype(jnp.bfloat16)
        gi_ref[rows, :] = lax.dot_general(
            agg, weight_ref[...], (((1,), (1,)), ((), ())),
            preferred_element_type=jnp.float32).astype(gi_ref.dtype)
        part = lax.dot_general(
            feat_ref[rows, :], agg, (((0,), (0,)), ((), ())),
            preferred_element_type=jnp.float32)

        @pl.when(c == 0)
        def _():
            wg_ref[...] = part

        @pl.when(c > 0)
        def _():
            wg_ref[...] += part

    wg_ref[...] = wg_ref[...] * scale


def slots(scale, index, count, src, edge, feat, weight):
    rows, width = feat.shape
    side = edge.shape[1]
    smem = pl.BlockSpec(memory_space=pltpu.SMEM)
    vmem = pl.BlockSpec(memory_space=pltpu.VMEM)
    return pl.pallas_call(
        lambda *refs: slots_kernel(scale, *refs),
        out_shape=(jax.ShapeDtypeStruct((rows, weight.shape[0]), jnp.bfloat16),
                   jax.ShapeDtypeStruct((width, src.shape[2]), jnp.float32)),
        in_specs=[smem, smem, vmem, vmem, vmem, vmem],
        out_specs=(vmem, vmem),
        scratch_shapes=[pltpu.VMEM((rows // side, side, src.shape[2]), jnp.float32)],
        compiler_params=pltpu.CompilerParams(vmem_limit_bytes=40 << 20),
        name="slots",
    )(index.reshape(-1), count, src, edge, feat, weight)


MESH = pl.DeviceIdType.MESH


def wrap(value, size):
    return lax.rem(value + 2 * size, size)


def regroup_kernel(zs_n, xs_n, ys_n, perm_ref, grad_ref, out_ref, ordered, raw, unperm,
                   own_sem, a_send, a_recv, y_send, y_recv, f_send, f_recv, p_send, p_recv):
    d = lax.axis_index("dom")
    r = lax.axis_index("rep")
    z, x = d // xs_n, lax.rem(d, xs_n)
    y, c = r // 2, lax.rem(r, 2)
    peers = zs_n * xs_n
    slot_rows = 4
    piece = 2 * ys_n * slot_rows
    r_up = wrap(y + 1, ys_n) * 2 + c
    r_down = wrap(y - 1, ys_n) * 2 + c
    r_far = wrap(y + 2, ys_n) * 2 + c
    r_pair = r + 1 - 2 * c

    def offset(j):
        return ((j + 1) // 2) * (2 * lax.rem(j, 2) - 1)

    barrier = pltpu.get_barrier_semaphore()

    @pl.loop(1, peers)
    def _(n):
        pl.semaphore_signal(barrier, inc=1, device_id={"dom": wrap(d + n, peers), "rep": r},
                            device_id_type=MESH)

    for other in (r_up, r_down, r_pair):
        pl.semaphore_signal(barrier, inc=1, device_id={"dom": d, "rep": other},
                            device_id_type=MESH)

    perm = perm_ref[...]
    target = (perm // grad_ref.shape[0]) * slot_rows + lax.rem(perm, slot_rows)
    tile = 256

    @pl.loop(0, grad_ref.shape[0] // tile)
    def _(t):
        rows = lax.broadcasted_iota(jnp.int32, (tile, grad_ref.shape[0]), 0) + t * tile
        hot = jnp.where(rows == target, 1.0, 0.0).astype(jnp.bfloat16)
        ordered[pl.ds(pl.multiple_of(t * tile, tile), tile), :] = lax.dot_general(
            hot, grad_ref[...], (((1,), (0,)), ((), ())),
            preferred_element_type=jnp.float32).astype(jnp.bfloat16)

    q = lax.broadcasted_iota(jnp.int32, (tile, tile), 0)
    p = lax.broadcasted_iota(jnp.int32, (tile, tile), 1)
    wanted = lax.rem(q // slot_rows, 8) * piece + (q // piece) * slot_rows + lax.rem(q, slot_rows)
    unperm[...] = jnp.where(p == wanted, 1.0, 0.0).astype(jnp.bfloat16)

    pl.semaphore_wait(barrier, peers - 1 + 3)

    own = pltpu.make_async_copy(
        ordered.at[pl.ds(pl.multiple_of(d * piece, piece), piece)], raw.at[z, x, r], own_sem)
    own.start()

    def a_copy(n, zs, xs):
        j, i = n // xs_n, lax.rem(n, xs_n)
        to = wrap(z + offset(j), zs_n) * xs_n + wrap(x + i, xs_n)
        return pltpu.make_async_remote_copy(
            src_ref=ordered.at[pl.ds(pl.multiple_of(to * piece, piece), piece)],
            dst_ref=raw.at[zs, xs, r],
            send_sem=a_send.at[n], recv_sem=a_recv.at[n],
            device_id={"dom": to, "rep": r}, device_id_type=MESH)

    @pl.loop(1, peers)
    def _(n):
        a_copy(n, z, x).start()

    def chunk_of(j):
        return wrap(z - offset(j), zs_n)

    def y_copy(j, way, owner):
        part = raw.at[chunk_of(j), :, owner]
        return pltpu.make_async_remote_copy(
            src_ref=part, dst_ref=part, send_sem=y_send.at[way, j], recv_sem=y_recv.at[way, j],
            device_id={"dom": d, "rep": (r_up, r_down)[way]}, device_id_type=MESH)

    half = xs_n // 2

    def f_copy(j, way, owner):
        part = raw.at[chunk_of(j), pl.ds(way * half, half), owner]
        return pltpu.make_async_remote_copy(
            src_ref=part, dst_ref=part, send_sem=f_send.at[way, j], recv_sem=f_recv.at[way, j],
            device_id={"dom": d, "rep": (r_up, r_down)[way]}, device_id_type=MESH)

    def p_copy(j, which, owner):
        part = raw.at[chunk_of(j), :, owner]
        return pltpu.make_async_remote_copy(
            src_ref=part, dst_ref=part, send_sem=p_send.at[which, j],
            recv_sem=p_recv.at[which, j],
            device_id={"dom": d, "rep": r_pair}, device_id_type=MESH)

    @pl.loop(0, zs_n + 3)
    def _(step):
        @pl.when(step < zs_n)
        def _():
            j = step

            @pl.when(j == 0)
            def _():
                own.wait()

            @pl.loop(0, xs_n)
            def _(i):
                @pl.when(j * xs_n + i > 0)
                def _():
                    a_copy(j * xs_n + i, chunk_of(j), wrap(x - i, xs_n)).wait_recv()

            y_copy(j, 0, r).start()
            y_copy(j, 1, r).start()
            p_copy(j, 0, r).start()

        @pl.when((step >= 1) & (step < zs_n + 1))
        def _():
            j = step - 1
            y_copy(j, 0, r_down).wait_recv()
            f_copy(j, 0, r_down).start()
            p_copy(j, 1, r_down).start()
            y_copy(j, 1, r_up).wait_recv()
            f_copy(j, 1, r_up).start()
            p_copy(j, 2, r_up).start()

        @pl.when((step >= 2) & (step < zs_n + 2))
        def _():
            j = step - 2
            f_copy(j, 0, r_far).wait_recv()
            f_copy(j, 1, r_far).wait_recv()
            p_copy(j, 3, r_far).start()

        @pl.when(step >= 3)
        def _():
            j = step - 3
            zs = chunk_of(j)
            flip = 1 - 2 * c
            p_copy(j, 0, r + flip).wait_recv()
            p_copy(j, 1, r_down + flip).wait_recv()
            p_copy(j, 2, r_up + flip).wait_recv()
            p_copy(j, 3, r_far + flip).wait_recv()
            for xs in range(xs_n):
                rows = raw[zs, xs].reshape(tile, out_ref.shape[-1])
                placed = lax.dot_general(
                    unperm[...], rows, (((1,), (0,)), ((), ())),
                    preferred_element_type=jnp.float32).astype(jnp.bfloat16)
                for t in range(2 * ys_n):
                    out_ref[t, zs, xs * piece:(xs + 1) * piece, :] = placed[
                        t * piece:(t + 1) * piece, :]

    @pl.loop(1, peers)
    def _(n):
        a_copy(n, z, x).wait_send()

    @pl.loop(0, zs_n)
    def _(j):
        for way in range(2):
            y_copy(j, way, r).wait_send()
            f_copy(j, way, r).wait_send()
        for which in range(4):
            p_copy(j, which, r).wait_send()


def regroup(perm, grad, sizes):
    zs_n, xs_n, ys_n = sizes
    rows, width = grad.shape
    reps, doms = 2 * ys_n, zs_n * xs_n
    piece = rows // doms
    vmem = pl.BlockSpec(memory_space=pltpu.VMEM)
    dma = pltpu.SemaphoreType.DMA
    return pl.pallas_call(
        lambda *refs: regroup_kernel(zs_n, xs_n, ys_n, *refs),
        out_shape=jax.ShapeDtypeStruct((reps, zs_n, rows // zs_n, width), grad.dtype),
        in_specs=[vmem, vmem],
        out_specs=vmem,
        scratch_shapes=[
            pltpu.VMEM((rows, width), grad.dtype),
            pltpu.VMEM((zs_n, xs_n, reps, piece, width), grad.dtype),
            pltpu.VMEM((256, 256), grad.dtype),
            dma, dma((doms,)), dma((doms,)),
            dma((2, zs_n)), dma((2, zs_n)), dma((2, zs_n)), dma((2, zs_n)),
            dma((4, zs_n)), dma((4, zs_n)),
        ],
        compiler_params=pltpu.CompilerParams(
            collective_id=0, has_side_effects=True, vmem_limit_bytes=32 << 20),
        name="regroup",
    )(perm.reshape(1, rows), grad)


def reduce_kernel(zs_n, xs_n, ys_n, part_ref, out_ref, pair_in, y_in, half_sum, cols_sum, dom_in,
                  result, c_send, c_recv, y_send, y_recv, d_send, d_recv, l_send, l_recv):
    d = lax.axis_index("dom")
    r = lax.axis_index("rep")
    y, c = r // 2, lax.rem(r, 2)
    doms = zs_n * xs_n
    group = doms // 2
    rows = out_ref.shape[0]
    lanes = 2 * out_ref.shape[1]
    tall = group * rows
    r_pair = r + 1 - 2 * c
    takes = d // group == c
    barrier = pltpu.get_barrier_semaphore()

    @pl.when(takes)
    def _():
        @pl.loop(1, doms)
        def _(n):
            pl.semaphore_signal(barrier, inc=1, device_id={"dom": wrap(d + n, doms), "rep": r},
                                device_id_type=MESH)

    @pl.loop(1, ys_n)
    def _(n):
        pl.semaphore_signal(barrier, inc=1,
                            device_id={"dom": d, "rep": wrap(y + n, ys_n) * 2 + c},
                            device_id_type=MESH)

    pl.semaphore_signal(barrier, inc=1, device_id={"dom": d, "rep": r_pair}, device_id_type=MESH)

    @pl.when(takes)
    def _():
        pl.semaphore_wait(barrier, group - 1 + ys_n)

    @pl.when(jnp.logical_not(takes))
    def _():
        pl.semaphore_wait(barrier, group + ys_n)

    def wide(n):
        return pl.ds(pl.multiple_of(wrap(y + n, ys_n) * lanes, lanes), lanes)

    order = (2, 1, 3, 0)
    mine = pl.ds(pl.multiple_of(c * tall, tall), tall)
    other = pl.ds(pl.multiple_of((1 - c) * tall, tall), tall)

    def c_copy(n):
        return pltpu.make_async_remote_copy(
            src_ref=part_ref.at[other, wide(n)], dst_ref=pair_in.at[n],
            send_sem=c_send.at[n], recv_sem=c_recv.at[n],
            device_id={"dom": d, "rep": r_pair}, device_id_type=MESH)

    def y_copy(n):
        return pltpu.make_async_remote_copy(
            src_ref=half_sum.at[n], dst_ref=y_in.at[n],
            send_sem=y_send.at[n], recv_sem=y_recv.at[n],
            device_id={"dom": d, "rep": wrap(y + n, ys_n) * 2 + c}, device_id_type=MESH)

    for n in order:
        c_copy(n).start()
    for n in order:
        c_copy(n).wait_recv()
        half_sum[n] = part_ref[mine, wide(n)] + pair_in[n]
        if n:
            y_copy(n).start()
    for n in (1, 3, 2):
        y_copy(n).wait_recv()
    cols_sum[...] = (half_sum[0] + y_in[1]) + (y_in[2] + y_in[3])

    def d_copy(n):
        return pltpu.make_async_remote_copy(
            src_ref=cols_sum.at[pl.ds(pl.multiple_of(n * rows, rows), rows)],
            dst_ref=dom_in.at[d],
            send_sem=d_send.at[n], recv_sem=d_recv.at[d],
            device_id={"dom": c * group + n, "rep": r}, device_id_type=MESH)

    @pl.loop(0, group)
    def _(m):
        n = lax.rem(m + d, group)

        @pl.when(c * group + n != d)
        def _():
            d_copy(n).start()

    def l_copy():
        return pltpu.make_async_remote_copy(
            src_ref=result, dst_ref=result, send_sem=l_send, recv_sem=l_recv,
            device_id={"dom": d, "rep": r_pair}, device_id_type=MESH)

    @pl.when(takes)
    def _():
        dom_in[d] = cols_sum[pl.ds(pl.multiple_of((d - c * group) * rows, rows), rows), :]

        @pl.loop(0, doms)
        def _(s):
            @pl.when(s != d)
            def _():
                pltpu.make_async_remote_copy(
                    src_ref=cols_sum.at[pl.ds(0, rows)], dst_ref=dom_in.at[s],
                    send_sem=d_send.at[0], recv_sem=d_recv.at[s],
                    device_id={"dom": d, "rep": r_pair}, device_id_type=MESH).wait_recv()

        total = dom_in[0]
        for s in range(1, doms):
            total = total + dom_in[s]
        result[...] = total
        l_copy().start()
        l_copy().wait_send()

    @pl.when(jnp.logical_not(takes))
    def _():
        l_copy().wait_recv()

    got = result[...]
    out_ref[...] = jnp.where(c == 0, got[:, : lanes // 2], got[:, lanes // 2 :])

    for n in order:
        c_copy(n).wait_send()
        if n:
            y_copy(n).wait_send()

    @pl.loop(0, group)
    def _(n):
        @pl.when(c * group + n != d)
        def _():
            d_copy(n).wait_send()


def reduce_parts(part, sizes):
    zs_n, xs_n, ys_n = sizes
    rows, cols = part.shape
    doms = zs_n * xs_n
    tall, lanes = rows // 2, cols // ys_n
    vmem = pl.BlockSpec(memory_space=pltpu.VMEM)
    dma = pltpu.SemaphoreType.DMA
    f32 = jnp.float32
    return pl.pallas_call(
        lambda *refs: reduce_kernel(zs_n, xs_n, ys_n, *refs),
        out_shape=jax.ShapeDtypeStruct((rows // doms, lanes // 2), f32),
        in_specs=[vmem],
        out_specs=vmem,
        scratch_shapes=[
            pltpu.VMEM((ys_n, tall, lanes), f32), pltpu.VMEM((ys_n, tall, lanes), f32),
            pltpu.VMEM((ys_n, tall, lanes), f32), pltpu.VMEM((tall, lanes), f32),
            pltpu.VMEM((doms, rows // doms, lanes), f32), pltpu.VMEM((rows // doms, lanes), f32),
            dma((ys_n,)), dma((ys_n,)), dma((ys_n,)), dma((ys_n,)),
            dma((doms // 2,)), dma((doms,)), dma, dma,
        ],
        compiler_params=pltpu.CompilerParams(collective_id=1, has_side_effects=True),
        name="reduce",
    )(part)


SIZES = (8, 4, 4)


def on_device(grad_out, features, weight, edge_blocks, block_index, block_count, node_perm):
    block_side = edge_blocks.shape[1]
    stacked = regroup(node_perm, grad_out, SIZES).reshape(-1, block_side, grad_out.shape[1])
    nodes = grad_out.shape[0] * lax.axis_size("dom") * lax.axis_size("rep")
    grad_input, partial = slots(
        1.0 / math.sqrt(nodes), block_index, block_count, stacked, edge_blocks, features, weight)
    return (grad_input, reduce_parts(partial, SIZES))


def solution(mesh):
    in_specs = (
        P(("dom", "rep"), None),
        P(("dom", "rep"), None),
        P(),
        P(("dom", "rep"), None, None),
        P(("dom", "rep"), None),
        P(("dom", "rep")),
        P(("dom", "rep")),
    )
    out_specs = (P(("dom", "rep"), None), P("dom", "rep"))
    return jax.shard_map(
        on_device, mesh=mesh, in_specs=in_specs, out_specs=out_specs, check_vma=False
    )
```

```python
import math

import jax
import jax.numpy as jnp
from jax import lax
from jax.experimental import pallas as pl
from jax.experimental.pallas import tpu as pltpu
from jax.sharding import PartitionSpec as P


def slots_kernel(scale, depth, step, table_ref, src_ref, edge_ref, feat_ref, weight_ref,
                 gi_ref, wg_ref, acc_ref, agg_ref, tab, tab_sem):
    side = edge_ref.shape[1]
    cols = agg_ref.shape[0] // side
    copy = pltpu.make_async_copy(table_ref, tab, tab_sem)
    copy.start()
    copy.wait()

    def product(first, count, end):
        edges, rows = [], []
        for g in range(count):
            p = first + g
            if end is not None and g > count - step:
                q = jnp.minimum(p, end - 1)
                e = edge_ref[tab[0, q]]
                e = jnp.where(p < end, e, jnp.zeros_like(e))
            else:
                q = p
                e = edge_ref[tab[0, q]]
            edges.append(e)
            rows.append(src_ref[tab[1, q]])
        return lax.dot_general(
            jnp.concatenate(edges, 0), jnp.concatenate(rows, 0), (((0,), (0,)), ((), ())),
            preferred_element_type=jnp.float32)

    @pl.loop(0, cols)
    def _(c):
        first = tab[2, c]
        end = tab[2, c + 1]
        count = end - first
        full = jnp.maximum(count - 1, 0) // depth
        rest = (count - full * depth + step - 1) // step
        tail = first + full * depth
        place = pl.ds(pl.multiple_of(c * side, side), side)
        acc_ref[...] = jnp.zeros_like(acc_ref)

        @pl.loop(0, full)
        def _(t):
            acc_ref[...] += product(first + t * depth, depth, None)

        @pl.when(rest == 0)
        def _():
            agg_ref[place, :] = jnp.zeros((side, agg_ref.shape[1]), agg_ref.dtype)

        for k in range(1, depth // step + 1):
            @pl.when(rest == k)
            def _():
                agg_ref[place, :] = (acc_ref[...] + product(tail, k * step, end)).astype(
                    agg_ref.dtype)

    wg_ref[...] = lax.dot_general(
        feat_ref[...], agg_ref[...], (((0,), (0,)), ((), ())),
        preferred_element_type=jnp.float32) * scale
    gi_ref[...] = lax.dot_general(
        agg_ref[...], weight_ref[...], (((1,), (1,)), ((), ())),
        preferred_element_type=jnp.float32).astype(gi_ref.dtype)


def slots(scale, table, src, edge, feat, weight):
    rows, width = feat.shape
    side = edge.shape[1]
    vmem = pl.BlockSpec(memory_space=pltpu.VMEM)
    return pl.pallas_call(
        lambda *refs: slots_kernel(scale, 16, 4, *refs),
        out_shape=(jax.ShapeDtypeStruct((rows, weight.shape[0]), jnp.bfloat16),
                   jax.ShapeDtypeStruct((width, src.shape[2]), jnp.float32)),
        in_specs=[vmem] * 5,
        out_specs=(vmem, vmem),
        scratch_shapes=[pltpu.VMEM((side, src.shape[2]), jnp.float32),
                        pltpu.VMEM((rows, src.shape[2]), jnp.bfloat16),
                        pltpu.SMEM(table.shape, jnp.int32),
                        pltpu.SemaphoreType.DMA],
        compiler_params=pltpu.CompilerParams(vmem_limit_bytes=20 << 20),
        name="slots",
    )(table, src, edge, feat, weight)


def slot_table(index, live):
    count = index.shape[1]
    here = lax.broadcasted_iota(jnp.int32, (count, count), 0)
    lane = lax.broadcasted_iota(jnp.int32, (count, count), 1)
    row = jnp.broadcast_to(index[0:1, :], (count, count)).astype(jnp.float32).T
    across = jnp.where(lane < live, jnp.broadcast_to(index[1:2, :], (count, count)), count)
    across = across.astype(jnp.float32)
    key = across.T
    ahead = (across < key) | ((across == key) & (lane < here))
    rank = jnp.sum(jnp.where(ahead, 1.0, 0.0), axis=1, keepdims=True)
    hit = rank == lane.astype(jnp.float32)
    slot = jnp.sum(jnp.where(hit, here.astype(jnp.float32), 0.0), axis=0, keepdims=True)
    block = jnp.sum(jnp.where(hit, row, 0.0), axis=0, keepdims=True)
    start = jnp.sum(jnp.where(key < lane.astype(jnp.float32), 1.0, 0.0), axis=0, keepdims=True)
    rest = jnp.zeros((5, count), jnp.float32)
    return jnp.concatenate([slot, block, start, rest], axis=0).astype(jnp.int32)


MESH = pl.DeviceIdType.MESH


def wrap(value, size):
    return lax.rem(value + 2 * size, size)


def regroup_kernel(zs_n, xs_n, ys_n, perm_hbm, grad_hbm, index_hbm, count_ref, out_ref,
                   table_ref, grad_ref, perm_ref, index_ref, load_sem, ordered, raw, unperm,
                   own_sem, a_send, a_recv, y_send, y_recv, f_send, f_recv, p_send, p_recv):
    d = lax.axis_index("dom")
    r = lax.axis_index("rep")
    z, x = d // xs_n, lax.rem(d, xs_n)
    y, c = r // 2, lax.rem(r, 2)
    peers = zs_n * xs_n
    slot_rows = 4
    piece = 2 * ys_n * slot_rows
    r_up = wrap(y + 1, ys_n) * 2 + c
    r_down = wrap(y - 1, ys_n) * 2 + c
    r_far = wrap(y + 2, ys_n) * 2 + c
    r_pair = r + 1 - 2 * c

    def offset(j):
        return ((j + 1) // 2) * (2 * lax.rem(j, 2) - 1)

    barrier = pltpu.get_barrier_semaphore()
    grad_load = pltpu.make_async_copy(grad_hbm, grad_ref, load_sem.at[0])
    grad_load.start()
    perm_load = pltpu.make_async_copy(perm_hbm, perm_ref, load_sem.at[1])
    perm_load.start()
    index_load = pltpu.make_async_copy(index_hbm, index_ref, load_sem.at[2])
    index_load.start()

    @pl.loop(1, peers)
    def _(n):
        pl.semaphore_signal(barrier, inc=1, device_id={"dom": wrap(d + n, peers), "rep": r},
                            device_id_type=MESH)

    for other in (r_up, r_down, r_pair):
        pl.semaphore_signal(barrier, inc=1, device_id={"dom": d, "rep": other},
                            device_id_type=MESH)

    perm_load.wait()
    perm = perm_ref[...]
    target = (perm // grad_ref.shape[0]) * slot_rows + lax.rem(perm, slot_rows)
    tile = 256
    grad_load.wait()

    @pl.loop(0, grad_ref.shape[0] // tile)
    def _(t):
        rows = lax.broadcasted_iota(jnp.int32, (tile, grad_ref.shape[0]), 0) + t * tile
        hot = jnp.where(rows == target, 1.0, 0.0).astype(jnp.bfloat16)
        ordered[pl.ds(pl.multiple_of(t * tile, tile), tile), :] = lax.dot_general(
            hot, grad_ref[...], (((1,), (0,)), ((), ())),
            preferred_element_type=jnp.float32).astype(jnp.bfloat16)

    pl.semaphore_wait(barrier, peers - 1 + 3)

    own = pltpu.make_async_copy(
        ordered.at[pl.ds(pl.multiple_of(d * piece, piece), piece)], raw.at[z, x, r], own_sem)
    own.start()

    def a_copy(n, zs, xs):
        j, i = n // xs_n, lax.rem(n, xs_n)
        to = wrap(z + offset(j), zs_n) * xs_n + wrap(x + i, xs_n)
        return pltpu.make_async_remote_copy(
            src_ref=ordered.at[pl.ds(pl.multiple_of(to * piece, piece), piece)],
            dst_ref=raw.at[zs, xs, r],
            send_sem=a_send.at[n], recv_sem=a_recv.at[n],
            device_id={"dom": to, "rep": r}, device_id_type=MESH)

    @pl.loop(1, peers)
    def _(n):
        a_copy(n, z, x).start()

    index_load.wait()
    table_ref[...] = slot_table(index_ref[...], count_ref[0])
    q = lax.broadcasted_iota(jnp.int32, (tile, tile), 0)
    p = lax.broadcasted_iota(jnp.int32, (tile, tile), 1)
    wanted = lax.rem(q // slot_rows, 8) * piece + (q // piece) * slot_rows + lax.rem(q, slot_rows)
    unperm[...] = jnp.where(p == wanted, 1.0, 0.0).astype(jnp.bfloat16)

    def chunk_of(j):
        return wrap(z - offset(j), zs_n)

    def y_copy(j, way, owner):
        part = raw.at[chunk_of(j), :, owner]
        return pltpu.make_async_remote_copy(
            src_ref=part, dst_ref=part, send_sem=y_send.at[way, j], recv_sem=y_recv.at[way, j],
            device_id={"dom": d, "rep": (r_up, r_down)[way]}, device_id_type=MESH)

    half = xs_n // 2

    def f_copy(j, way, owner):
        part = raw.at[chunk_of(j), pl.ds(way * half, half), owner]
        return pltpu.make_async_remote_copy(
            src_ref=part, dst_ref=part, send_sem=f_send.at[way, j], recv_sem=f_recv.at[way, j],
            device_id={"dom": d, "rep": (r_up, r_down)[way]}, device_id_type=MESH)

    def p_copy(j, which, owner):
        part = raw.at[chunk_of(j), :, owner]
        return pltpu.make_async_remote_copy(
            src_ref=part, dst_ref=part, send_sem=p_send.at[which, j],
            recv_sem=p_recv.at[which, j],
            device_id={"dom": d, "rep": r_pair}, device_id_type=MESH)

    @pl.loop(0, zs_n + 3)
    def _(step):
        @pl.when(step < zs_n)
        def _():
            j = step

            @pl.when(j == 0)
            def _():
                own.wait()

            @pl.loop(0, xs_n)
            def _(i):
                @pl.when(j * xs_n + i > 0)
                def _():
                    a_copy(j * xs_n + i, chunk_of(j), wrap(x - i, xs_n)).wait_recv()

            y_copy(j, 0, r).start()
            y_copy(j, 1, r).start()
            p_copy(j, 0, r).start()

        @pl.when((step >= 1) & (step < zs_n + 1))
        def _():
            j = step - 1
            y_copy(j, 0, r_down).wait_recv()
            f_copy(j, 0, r_down).start()
            p_copy(j, 1, r_down).start()
            y_copy(j, 1, r_up).wait_recv()
            f_copy(j, 1, r_up).start()
            p_copy(j, 2, r_up).start()

        @pl.when((step >= 2) & (step < zs_n + 2))
        def _():
            j = step - 2
            f_copy(j, 0, r_far).wait_recv()
            f_copy(j, 1, r_far).wait_recv()
            p_copy(j, 3, r_far).start()

        @pl.when(step >= 3)
        def _():
            j = step - 3
            zs = chunk_of(j)
            flip = 1 - 2 * c
            p_copy(j, 0, r + flip).wait_recv()
            p_copy(j, 1, r_down + flip).wait_recv()
            p_copy(j, 2, r_up + flip).wait_recv()
            p_copy(j, 3, r_far + flip).wait_recv()
            for xs in range(xs_n):
                rows = raw[zs, xs].reshape(tile, out_ref.shape[-1])
                placed = lax.dot_general(
                    unperm[...], rows, (((1,), (0,)), ((), ())),
                    preferred_element_type=jnp.float32).astype(jnp.bfloat16)
                for t in range(2 * ys_n):
                    out_ref[t, zs, xs * piece:(xs + 1) * piece, :] = placed[
                        t * piece:(t + 1) * piece, :]

    @pl.loop(1, peers)
    def _(n):
        a_copy(n, z, x).wait_send()

    @pl.loop(0, zs_n)
    def _(j):
        for way in range(2):
            y_copy(j, way, r).wait_send()
            f_copy(j, way, r).wait_send()
        for which in range(4):
            p_copy(j, which, r).wait_send()


def regroup(perm, grad, index, count, sizes):
    zs_n, xs_n, ys_n = sizes
    rows, width = grad.shape
    reps, doms = 2 * ys_n, zs_n * xs_n
    piece = rows // doms
    vmem = pl.BlockSpec(memory_space=pltpu.VMEM)
    dma = pltpu.SemaphoreType.DMA
    far = pl.BlockSpec(memory_space=pltpu.HBM)
    return pl.pallas_call(
        lambda *refs: regroup_kernel(zs_n, xs_n, ys_n, *refs),
        out_shape=(jax.ShapeDtypeStruct((reps, zs_n, rows // zs_n, width), grad.dtype),
                   jax.ShapeDtypeStruct((8, index.shape[1]), jnp.int32)),
        in_specs=[far, far, far, pl.BlockSpec(memory_space=pltpu.SMEM)],
        out_specs=(vmem, vmem),
        cost_estimate=pl.CostEstimate(flops=40*10**9, bytes_accessed=150*10**6, transcendentals=0),
        scratch_shapes=[
            pltpu.VMEM((rows, width), grad.dtype), pltpu.VMEM((1, rows), jnp.int32),
            pltpu.VMEM(index.shape, jnp.int32), dma((3,)),
            pltpu.VMEM((rows, width), grad.dtype),
            pltpu.VMEM((zs_n, xs_n, reps, piece, width), grad.dtype),
            pltpu.VMEM((256, 256), grad.dtype),
            dma, dma((doms,)), dma((doms,)),
            dma((2, zs_n)), dma((2, zs_n)), dma((2, zs_n)), dma((2, zs_n)),
            dma((4, zs_n)), dma((4, zs_n)),
        ],
        compiler_params=pltpu.CompilerParams(
            collective_id=0, has_side_effects=True, vmem_limit_bytes=14 << 20),
        name="regroup",
    )(perm.reshape(1, rows), grad, index, count)


def reduce_kernel(zs_n, xs_n, ys_n, part_ref, out_ref, pair_in, y_in, half_sum, cols_sum, dom_in,
                  result, c_send, c_recv, y_send, y_recv, d_send, d_recv, l_send, l_recv):
    d = lax.axis_index("dom")
    r = lax.axis_index("rep")
    y, c = r // 2, lax.rem(r, 2)
    doms = zs_n * xs_n
    group = doms // 2
    rows = out_ref.shape[0]
    lanes = 2 * out_ref.shape[1]
    tall = group * rows
    r_pair = r + 1 - 2 * c
    takes = d // group == c
    barrier = pltpu.get_barrier_semaphore()

    @pl.when(takes)
    def _():
        @pl.loop(1, doms)
        def _(n):
            pl.semaphore_signal(barrier, inc=1, device_id={"dom": wrap(d + n, doms), "rep": r},
                                device_id_type=MESH)

    @pl.loop(1, ys_n)
    def _(n):
        pl.semaphore_signal(barrier, inc=1,
                            device_id={"dom": d, "rep": wrap(y + n, ys_n) * 2 + c},
                            device_id_type=MESH)

    pl.semaphore_signal(barrier, inc=1, device_id={"dom": d, "rep": r_pair}, device_id_type=MESH)

    @pl.when(takes)
    def _():
        pl.semaphore_wait(barrier, group - 1 + ys_n)

    @pl.when(jnp.logical_not(takes))
    def _():
        pl.semaphore_wait(barrier, group + ys_n)

    def wide(n):
        return pl.ds(pl.multiple_of(wrap(y + n, ys_n) * lanes, lanes), lanes)

    order = (2, 1, 3, 0)
    mine = pl.ds(pl.multiple_of(c * tall, tall), tall)
    other = pl.ds(pl.multiple_of((1 - c) * tall, tall), tall)

    def c_copy(n):
        return pltpu.make_async_remote_copy(
            src_ref=part_ref.at[other, wide(n)], dst_ref=pair_in.at[n],
            send_sem=c_send.at[n], recv_sem=c_recv.at[n],
            device_id={"dom": d, "rep": r_pair}, device_id_type=MESH)

    def y_copy(n):
        return pltpu.make_async_remote_copy(
            src_ref=half_sum.at[n], dst_ref=y_in.at[n],
            send_sem=y_send.at[n], recv_sem=y_recv.at[n],
            device_id={"dom": d, "rep": wrap(y + n, ys_n) * 2 + c}, device_id_type=MESH)

    for n in order:
        c_copy(n).start()
    for n in order:
        c_copy(n).wait_recv()
        half_sum[n] = part_ref[mine, wide(n)] + pair_in[n]
        if n:
            y_copy(n).start()
    for n in (1, 3, 2):
        y_copy(n).wait_recv()
    cols_sum[...] = (half_sum[0] + y_in[1]) + (y_in[2] + y_in[3])

    def d_copy(n):
        return pltpu.make_async_remote_copy(
            src_ref=cols_sum.at[pl.ds(pl.multiple_of(n * rows, rows), rows)],
            dst_ref=dom_in.at[d],
            send_sem=d_send.at[n], recv_sem=d_recv.at[d],
            device_id={"dom": c * group + n, "rep": r}, device_id_type=MESH)

    @pl.loop(0, group)
    def _(m):
        n = lax.rem(m + d, group)

        @pl.when(c * group + n != d)
        def _():
            d_copy(n).start()

    def l_copy():
        return pltpu.make_async_remote_copy(
            src_ref=result, dst_ref=result, send_sem=l_send, recv_sem=l_recv,
            device_id={"dom": d, "rep": r_pair}, device_id_type=MESH)

    @pl.when(takes)
    def _():
        dom_in[d] = cols_sum[pl.ds(pl.multiple_of((d - c * group) * rows, rows), rows), :]

        @pl.loop(0, doms)
        def _(s):
            @pl.when(s != d)
            def _():
                pltpu.make_async_remote_copy(
                    src_ref=cols_sum.at[pl.ds(0, rows)], dst_ref=dom_in.at[s],
                    send_sem=d_send.at[0], recv_sem=d_recv.at[s],
                    device_id={"dom": d, "rep": r_pair}, device_id_type=MESH).wait_recv()

        total = dom_in[0]
        for s in range(1, doms):
            total = total + dom_in[s]
        result[...] = total
        l_copy().start()
        l_copy().wait_send()

    @pl.when(jnp.logical_not(takes))
    def _():
        l_copy().wait_recv()

    got = result[...]
    out_ref[...] = jnp.where(c == 0, got[:, : lanes // 2], got[:, lanes // 2 :])

    for n in order:
        c_copy(n).wait_send()
        if n:
            y_copy(n).wait_send()

    @pl.loop(0, group)
    def _(n):
        @pl.when(c * group + n != d)
        def _():
            d_copy(n).wait_send()


def reduce_parts(part, sizes):
    zs_n, xs_n, ys_n = sizes
    rows, cols = part.shape
    doms = zs_n * xs_n
    tall, lanes = rows // 2, cols // ys_n
    vmem = pl.BlockSpec(memory_space=pltpu.VMEM)
    dma = pltpu.SemaphoreType.DMA
    f32 = jnp.float32
    return pl.pallas_call(
        lambda *refs: reduce_kernel(zs_n, xs_n, ys_n, *refs),
        out_shape=jax.ShapeDtypeStruct((rows // doms, lanes // 2), f32),
        in_specs=[vmem],
        out_specs=vmem,
        scratch_shapes=[
            pltpu.VMEM((ys_n, tall, lanes), f32), pltpu.VMEM((ys_n, tall, lanes), f32),
            pltpu.VMEM((ys_n, tall, lanes), f32), pltpu.VMEM((tall, lanes), f32),
            pltpu.VMEM((doms, rows // doms, lanes), f32), pltpu.VMEM((rows // doms, lanes), f32),
            dma((ys_n,)), dma((ys_n,)), dma((ys_n,)), dma((ys_n,)),
            dma((doms // 2,)), dma((doms,)), dma, dma,
        ],
        compiler_params=pltpu.CompilerParams(
            collective_id=1, has_side_effects=True, vmem_limit_bytes=8 << 20),
        name="reduce",
    )(part)


SIZES = (8, 4, 4)


def on_device(grad_out, features, weight, edge_blocks, block_index, block_count, node_perm):
    block_side = edge_blocks.shape[1]
    stacked, table = regroup(node_perm, grad_out, block_index.T, block_count, SIZES)
    stacked = stacked.reshape(-1, block_side, grad_out.shape[1])
    nodes = grad_out.shape[0] * lax.axis_size("dom") * lax.axis_size("rep")
    grad_input, partial = slots(
        1.0 / math.sqrt(nodes), table, stacked, edge_blocks, features, weight)
    return (grad_input, reduce_parts(partial, SIZES))


def solution(mesh):
    in_specs = (
        P(("dom", "rep"), None),
        P(("dom", "rep"), None),
        P(),
        P(("dom", "rep"), None, None),
        P(("dom", "rep"), None),
        P(("dom", "rep")),
        P(("dom", "rep")),
    )
    out_specs = (P(("dom", "rep"), None), P("dom", "rep"))
    return jax.shard_map(
        on_device, mesh=mesh, in_specs=in_specs, out_specs=out_specs, check_vma=False
    )
```

```python
import math

import jax
import jax.numpy as jnp
from jax import lax
from jax.experimental import pallas as pl
from jax.experimental.pallas import tpu as pltpu
from jax.sharding import PartitionSpec as P


def slots_kernel(depth, step, table_ref, src_ref, edge_ref, weight_ref,
                 gi_ref, agg_ref, acc_ref, tab, tab_sem):
    side = edge_ref.shape[1]
    cols = agg_ref.shape[0] // side
    copy = pltpu.make_async_copy(table_ref, tab, tab_sem)
    copy.start()
    copy.wait()

    def product(first, count, end):
        edges, rows = [], []
        for g in range(count):
            p = first + g
            if end is not None and g > count - step:
                q = jnp.minimum(p, end - 1)
                e = edge_ref[tab[0, q]]
                e = jnp.where(p < end, e, jnp.zeros_like(e))
            else:
                q = p
                e = edge_ref[tab[0, q]]
            edges.append(e)
            rows.append(src_ref[tab[1, q]])
        return lax.dot_general(
            jnp.concatenate(edges, 0), jnp.concatenate(rows, 0), (((0,), (0,)), ((), ())),
            preferred_element_type=jnp.float32)

    @pl.loop(0, cols)
    def _(c):
        first = tab[2, c]
        end = tab[2, c + 1]
        count = end - first
        full = jnp.maximum(count - 1, 0) // depth
        rest = (count - full * depth + step - 1) // step
        tail = first + full * depth
        place = pl.ds(pl.multiple_of(c * side, side), side)
        acc_ref[...] = jnp.zeros_like(acc_ref)

        @pl.loop(0, full)
        def _(t):
            acc_ref[...] += product(first + t * depth, depth, None)

        @pl.when(rest == 0)
        def _():
            agg_ref[place, :] = jnp.zeros((side, agg_ref.shape[1]), agg_ref.dtype)

        for k in range(1, depth // step + 1):
            @pl.when(rest == k)
            def _():
                agg_ref[place, :] = (acc_ref[...] + product(tail, k * step, end)).astype(
                    agg_ref.dtype)

    gi_ref[...] = lax.dot_general(
        agg_ref[...], weight_ref[...], (((1,), (1,)), ((), ())),
        preferred_element_type=jnp.float32).astype(gi_ref.dtype)


def slots(table, src, edge, weight):
    side = edge.shape[1]
    rows = src.shape[0] * side // 8
    vmem = pl.BlockSpec(memory_space=pltpu.VMEM)
    return pl.pallas_call(
        lambda *refs: slots_kernel(16, 4, *refs),
        out_shape=(jax.ShapeDtypeStruct((rows, weight.shape[0]), jnp.bfloat16),
                   jax.ShapeDtypeStruct((rows, src.shape[2]), jnp.bfloat16)),
        in_specs=[vmem] * 4,
        out_specs=(vmem, vmem),
        scratch_shapes=[pltpu.VMEM((side, src.shape[2]), jnp.float32),
                        pltpu.SMEM(table.shape, jnp.int32),
                        pltpu.SemaphoreType.DMA],
        compiler_params=pltpu.CompilerParams(vmem_limit_bytes=20 << 20),
        name="slots",
    )(table, src, edge, weight)


def slot_table(index, live):
    count = index.shape[1]
    here = lax.broadcasted_iota(jnp.int32, (count, count), 0)
    lane = lax.broadcasted_iota(jnp.int32, (count, count), 1)
    row = jnp.broadcast_to(index[0:1, :], (count, count)).astype(jnp.float32).T
    across = jnp.where(lane < live, jnp.broadcast_to(index[1:2, :], (count, count)), count)
    across = across.astype(jnp.float32)
    key = across.T
    ahead = (across < key) | ((across == key) & (lane < here))
    rank = jnp.sum(jnp.where(ahead, 1.0, 0.0), axis=1, keepdims=True)
    hit = rank == lane.astype(jnp.float32)
    slot = jnp.sum(jnp.where(hit, here.astype(jnp.float32), 0.0), axis=0, keepdims=True)
    block = jnp.sum(jnp.where(hit, row, 0.0), axis=0, keepdims=True)
    start = jnp.sum(jnp.where(key < lane.astype(jnp.float32), 1.0, 0.0), axis=0, keepdims=True)
    rest = jnp.zeros((5, count), jnp.float32)
    return jnp.concatenate([slot, block, start, rest], axis=0).astype(jnp.int32)


MESH = pl.DeviceIdType.MESH


def wrap(value, size):
    return lax.rem(value + 2 * size, size)


def regroup_kernel(zs_n, xs_n, ys_n, perm_hbm, grad_hbm, index_hbm, count_ref, out_ref,
                   table_ref, grad_ref, perm_ref, index_ref, load_sem, ordered, raw, unperm,
                   own_sem, a_send, a_recv, y_send, y_recv, f_send, f_recv, p_send, p_recv):
    d = lax.axis_index("dom")
    r = lax.axis_index("rep")
    z, x = d // xs_n, lax.rem(d, xs_n)
    y, c = r // 2, lax.rem(r, 2)
    peers = zs_n * xs_n
    slot_rows = 4
    piece = 2 * ys_n * slot_rows
    r_up = wrap(y + 1, ys_n) * 2 + c
    r_down = wrap(y - 1, ys_n) * 2 + c
    r_far = wrap(y + 2, ys_n) * 2 + c
    r_pair = r + 1 - 2 * c

    def offset(j):
        return ((j + 1) // 2) * (2 * lax.rem(j, 2) - 1)

    barrier = pltpu.get_barrier_semaphore()
    grad_load = pltpu.make_async_copy(grad_hbm, grad_ref, load_sem.at[0])
    grad_load.start()
    perm_load = pltpu.make_async_copy(perm_hbm, perm_ref, load_sem.at[1])
    perm_load.start()
    index_load = pltpu.make_async_copy(index_hbm, index_ref, load_sem.at[2])
    index_load.start()

    @pl.loop(1, peers)
    def _(n):
        pl.semaphore_signal(barrier, inc=1, device_id={"dom": wrap(d + n, peers), "rep": r},
                            device_id_type=MESH)

    for other in (r_up, r_down, r_pair):
        pl.semaphore_signal(barrier, inc=1, device_id={"dom": d, "rep": other},
                            device_id_type=MESH)

    perm_load.wait()
    perm = perm_ref[...]
    target = (perm // grad_ref.shape[0]) * slot_rows + lax.rem(perm, slot_rows)
    tile = 256
    grad_load.wait()

    @pl.loop(0, grad_ref.shape[0] // tile)
    def _(t):
        rows = lax.broadcasted_iota(jnp.int32, (tile, grad_ref.shape[0]), 0) + t * tile
        hot = jnp.where(rows == target, 1.0, 0.0).astype(jnp.bfloat16)
        ordered[pl.ds(pl.multiple_of(t * tile, tile), tile), :] = lax.dot_general(
            hot, grad_ref[...], (((1,), (0,)), ((), ())),
            preferred_element_type=jnp.float32).astype(jnp.bfloat16)

    pl.semaphore_wait(barrier, peers - 1 + 3)

    own = pltpu.make_async_copy(
        ordered.at[pl.ds(pl.multiple_of(d * piece, piece), piece)], raw.at[z, x, r], own_sem)
    own.start()

    def a_copy(n, zs, xs):
        j, i = n // xs_n, lax.rem(n, xs_n)
        to = wrap(z + offset(j), zs_n) * xs_n + wrap(x + i, xs_n)
        return pltpu.make_async_remote_copy(
            src_ref=ordered.at[pl.ds(pl.multiple_of(to * piece, piece), piece)],
            dst_ref=raw.at[zs, xs, r],
            send_sem=a_send.at[n], recv_sem=a_recv.at[n],
            device_id={"dom": to, "rep": r}, device_id_type=MESH)

    @pl.loop(1, peers)
    def _(n):
        a_copy(n, z, x).start()

    index_load.wait()
    table_ref[...] = slot_table(index_ref[...], count_ref[0])
    q = lax.broadcasted_iota(jnp.int32, (tile, tile), 0)
    p = lax.broadcasted_iota(jnp.int32, (tile, tile), 1)
    wanted = lax.rem(q // slot_rows, 8) * piece + (q // piece) * slot_rows + lax.rem(q, slot_rows)
    unperm[...] = jnp.where(p == wanted, 1.0, 0.0).astype(jnp.bfloat16)

    def chunk_of(j):
        return wrap(z - offset(j), zs_n)

    def y_copy(j, way, owner):
        part = raw.at[chunk_of(j), :, owner]
        return pltpu.make_async_remote_copy(
            src_ref=part, dst_ref=part, send_sem=y_send.at[way, j], recv_sem=y_recv.at[way, j],
            device_id={"dom": d, "rep": (r_up, r_down)[way]}, device_id_type=MESH)

    half = xs_n // 2

    def f_copy(j, way, owner):
        part = raw.at[chunk_of(j), pl.ds(way * half, half), owner]
        return pltpu.make_async_remote_copy(
            src_ref=part, dst_ref=part, send_sem=f_send.at[way, j], recv_sem=f_recv.at[way, j],
            device_id={"dom": d, "rep": (r_up, r_down)[way]}, device_id_type=MESH)

    def p_copy(j, which, owner):
        part = raw.at[chunk_of(j), :, owner]
        return pltpu.make_async_remote_copy(
            src_ref=part, dst_ref=part, send_sem=p_send.at[which, j],
            recv_sem=p_recv.at[which, j],
            device_id={"dom": d, "rep": r_pair}, device_id_type=MESH)

    @pl.loop(0, zs_n + 3)
    def _(step):
        @pl.when(step < zs_n)
        def _():
            j = step

            @pl.when(j == 0)
            def _():
                own.wait()

            @pl.loop(0, xs_n)
            def _(i):
                @pl.when(j * xs_n + i > 0)
                def _():
                    a_copy(j * xs_n + i, chunk_of(j), wrap(x - i, xs_n)).wait_recv()

            y_copy(j, 0, r).start()
            y_copy(j, 1, r).start()
            p_copy(j, 0, r).start()

        @pl.when((step >= 1) & (step < zs_n + 1))
        def _():
            j = step - 1
            y_copy(j, 0, r_down).wait_recv()
            f_copy(j, 0, r_down).start()
            p_copy(j, 1, r_down).start()
            y_copy(j, 1, r_up).wait_recv()
            f_copy(j, 1, r_up).start()
            p_copy(j, 2, r_up).start()

        @pl.when((step >= 2) & (step < zs_n + 2))
        def _():
            j = step - 2
            f_copy(j, 0, r_far).wait_recv()
            f_copy(j, 1, r_far).wait_recv()
            p_copy(j, 3, r_far).start()

        @pl.when(step >= 3)
        def _():
            j = step - 3
            zs = chunk_of(j)
            flip = 1 - 2 * c
            p_copy(j, 0, r + flip).wait_recv()
            p_copy(j, 1, r_down + flip).wait_recv()
            p_copy(j, 2, r_up + flip).wait_recv()
            p_copy(j, 3, r_far + flip).wait_recv()
            for xs in range(xs_n):
                rows = raw[zs, xs].reshape(tile, out_ref.shape[-1])
                placed = lax.dot_general(
                    unperm[...], rows, (((1,), (0,)), ((), ())),
                    preferred_element_type=jnp.float32).astype(jnp.bfloat16)
                for t in range(2 * ys_n):
                    out_ref[t, zs, xs * piece:(xs + 1) * piece, :] = placed[
                        t * piece:(t + 1) * piece, :]

    @pl.loop(1, peers)
    def _(n):
        a_copy(n, z, x).wait_send()

    @pl.loop(0, zs_n)
    def _(j):
        for way in range(2):
            y_copy(j, way, r).wait_send()
            f_copy(j, way, r).wait_send()
        for which in range(4):
            p_copy(j, which, r).wait_send()


def regroup(perm, grad, index, count, sizes):
    zs_n, xs_n, ys_n = sizes
    rows, width = grad.shape
    reps, doms = 2 * ys_n, zs_n * xs_n
    piece = rows // doms
    vmem = pl.BlockSpec(memory_space=pltpu.VMEM)
    dma = pltpu.SemaphoreType.DMA
    far = pl.BlockSpec(memory_space=pltpu.HBM)
    return pl.pallas_call(
        lambda *refs: regroup_kernel(zs_n, xs_n, ys_n, *refs),
        out_shape=(jax.ShapeDtypeStruct((reps, zs_n, rows // zs_n, width), grad.dtype),
                   jax.ShapeDtypeStruct((8, index.shape[1]), jnp.int32)),
        in_specs=[far, far, far, pl.BlockSpec(memory_space=pltpu.SMEM)],
        out_specs=(vmem, vmem),
        cost_estimate=pl.CostEstimate(flops=40*10**9, bytes_accessed=150*10**6, transcendentals=0),
        scratch_shapes=[
            pltpu.VMEM((rows, width), grad.dtype), pltpu.VMEM((1, rows), jnp.int32),
            pltpu.VMEM(index.shape, jnp.int32), dma((3,)),
            pltpu.VMEM((rows, width), grad.dtype),
            pltpu.VMEM((zs_n, xs_n, reps, piece, width), grad.dtype),
            pltpu.VMEM((256, 256), grad.dtype),
            dma, dma((doms,)), dma((doms,)),
            dma((2, zs_n)), dma((2, zs_n)), dma((2, zs_n)), dma((2, zs_n)),
            dma((4, zs_n)), dma((4, zs_n)),
        ],
        compiler_params=pltpu.CompilerParams(
            collective_id=0, has_side_effects=True, vmem_limit_bytes=14 << 20),
        name="regroup",
    )(perm.reshape(1, rows), grad, index, count)


def reduce_kernel(zs_n, xs_n, ys_n, scale, stage, agg_ref, feat_ref, out_ref, part_other, part_mine,
                  pair_in, sums, far_in, y_in, cols_sum, packed, dom_in,
                  c_send, c_recv, s_send, s_recv, y_send, y_recv, d_send, d_recv):
    d = lax.axis_index("dom")
    r = lax.axis_index("rep")
    y, c = r // 2, lax.rem(r, 2)
    doms = zs_n * xs_n
    group = doms // 2
    rows = out_ref.shape[0]
    tall, lanes = cols_sum.shape
    mid = tall // 2
    r_pair = r + 1 - 2 * c
    r_way = (wrap(y + 1, ys_n) * 2 + c, wrap(y - 1, ys_n) * 2 + c)
    home = d // group
    barrier = pltpu.get_barrier_semaphore()

    for other in (*r_way, r_pair):
        pl.semaphore_signal(barrier, inc=1, device_id={"dom": d, "rep": other},
                            device_id_type=MESH)

    @pl.loop(0, doms)
    def _(n):
        @pl.when((n > 0) | (c != home))
        def _():
            pl.semaphore_signal(barrier, inc=1,
                                device_id={"dom": wrap(d + n, doms), "rep": y * 2 + home},
                                device_id_type=MESH)

    def partial(half):
        cols = feat_ref[:, pl.ds(pl.multiple_of(half * tall, tall), tall)]
        return lax.dot_general(
            cols, agg_ref[...], (((0,), (0,)), ((), ())),
            preferred_element_type=jnp.float32) * scale

    part_other[...] = partial(1 - c)

    @pl.when(c == home)
    def _():
        pl.semaphore_wait(barrier, doms - 1 + 3)

    @pl.when(c != home)
    def _():
        pl.semaphore_wait(barrier, doms + 3)

    def wide(n):
        return pl.ds(pl.multiple_of(wrap(y + n, ys_n) * lanes, lanes), lanes)

    def c_copy(n):
        return pltpu.make_async_remote_copy(
            src_ref=part_other.at[:, wide(n)], dst_ref=pair_in.at[n],
            send_sem=c_send.at[n], recv_sem=c_recv.at[n],
            device_id={"dom": d, "rep": r_pair}, device_id_type=MESH)

    def s_copy(way):
        return pltpu.make_async_remote_copy(
            src_ref=sums.at[2, pl.ds(way * mid, mid)], dst_ref=far_in.at[way],
            send_sem=s_send.at[way], recv_sem=s_recv.at[way],
            device_id={"dom": d, "rep": r_way[way]}, device_id_type=MESH)

    def y_copy(way, part):
        place = pl.ds(part * mid, mid)
        return pltpu.make_async_remote_copy(
            src_ref=sums.at[1 + 2 * way, place], dst_ref=y_in.at[way, place],
            send_sem=y_send.at[way, part], recv_sem=y_recv.at[way, part],
            device_id={"dom": d, "rep": r_way[way]}, device_id_type=MESH)

    def add_pair(n):
        c_copy(n).wait_recv()
        sums[n] = part_mine[:, wide(n)] + pair_in[n]

    if stage >= 1:
        for n in (2, 1, 3, 0):
            c_copy(n).start()
        part_mine[...] = partial(c)
        add_pair(2)
        if stage >= 2:
            for way in range(2):
                s_copy(way).start()
        for way in range(2):
            add_pair(1 + 2 * way)
            if stage >= 2:
                y_copy(way, 1 - way).start()
        add_pair(0)
    if stage >= 2:
        for way in range(2):
            s_copy(way).wait_recv()
            sums[1 + 2 * way, way * mid:(way + 1) * mid] += far_in[way]
            y_copy(way, way).start()
        for way in range(2):
            y_copy(way, 1 - way).wait_recv()
        for way in range(2):
            y_copy(way, way).wait_recv()
        cols_sum[...] = sums[0] + (y_in[0] + y_in[1])
    both = cols_sum[...].reshape(group, rows, lanes)
    low, high = both[:, :rows // 2], both[:, rows // 2:]
    left = lax.broadcasted_iota(jnp.int32, low.shape, 2) < lanes // 2
    packed[0] = jnp.where(left, low, pltpu.roll(high, lanes // 2, 2))
    packed[1] = jnp.where(left, pltpu.roll(low, lanes // 2, 2), high)

    def d_copy(n, core):
        return pltpu.make_async_remote_copy(
            src_ref=packed.at[core, n], dst_ref=dom_in.at[d],
            send_sem=d_send.at[core, n], recv_sem=d_recv.at[d],
            device_id={"dom": c * group + n, "rep": y * 2 + core}, device_id_type=MESH)

    if stage >= 3:
        @pl.loop(0, group)
        def _(m):
            n = lax.rem(m + d + group // 2, group)
            for core in range(2):
                @pl.when((c * group + n != d) | (c != core))
                def _():
                    d_copy(n, core).start()

        @pl.when(c == home)
        def _():
            dom_in[d] = packed[c, d - c * group]

        @pl.loop(0, doms)
        def _(s):
            @pl.when((s != d) | (c != home))
            def _():
                pltpu.make_async_remote_copy(
                    src_ref=packed.at[0, 0], dst_ref=dom_in.at[s],
                    send_sem=d_send.at[0, 0], recv_sem=d_recv.at[s],
                    device_id={"dom": d, "rep": r_pair}, device_id_type=MESH).wait_recv()

    sums_of = [dom_in[s] for s in range(doms)]
    while len(sums_of) > 1:
        sums_of = [a + b for a, b in zip(sums_of[::2], sums_of[1::2])]
    total = sums_of[0]
    out_ref[:rows // 2] = total[:, :lanes // 2]
    out_ref[rows // 2:] = total[:, lanes // 2:]

    if stage >= 1:
        for n in range(ys_n):
            c_copy(n).wait_send()
    if stage >= 2:
        for way in range(2):
            s_copy(way).wait_send()
            for part in range(2):
                y_copy(way, part).wait_send()
    if stage >= 3:
        @pl.loop(0, group)
        def _(n):
            for core in range(2):
                @pl.when((c * group + n != d) | (c != core))
                def _():
                    d_copy(n, core).wait_send()


def reduce_parts(scale, agg, feat, sizes, stage=3):
    zs_n, xs_n, ys_n = sizes
    rows, cols = feat.shape[1], agg.shape[1]
    doms = zs_n * xs_n
    tall, lanes = rows // 2, cols // ys_n
    vmem = pl.BlockSpec(memory_space=pltpu.VMEM)
    dma = pltpu.SemaphoreType.DMA
    f32 = jnp.float32
    return pl.pallas_call(
        lambda *refs: reduce_kernel(zs_n, xs_n, ys_n, scale, stage, *refs),
        out_shape=jax.ShapeDtypeStruct((rows // doms, lanes // 2), f32),
        in_specs=[vmem, vmem],
        out_specs=vmem,
        scratch_shapes=[
            pltpu.VMEM((tall, cols), f32), pltpu.VMEM((tall, cols), f32),
            pltpu.VMEM((ys_n, tall, lanes), f32), pltpu.VMEM((ys_n, tall, lanes), f32),
            pltpu.VMEM((2, tall // 2, lanes), f32), pltpu.VMEM((2, tall, lanes), f32),
            pltpu.VMEM((tall, lanes), f32),
            pltpu.VMEM((2, doms // 2, rows // doms // 2, lanes), f32),
            pltpu.VMEM((doms, rows // doms // 2, lanes), f32),
            dma((ys_n,)), dma((ys_n,)), dma((2,)), dma((2,)), dma((2, 2)), dma((2, 2)),
            dma((2, doms // 2)), dma((doms,)),
        ],
        compiler_params=pltpu.CompilerParams(
            collective_id=1, has_side_effects=True, vmem_limit_bytes=12 << 20),
        name="reduce",
    )(agg, feat)


SIZES = (8, 4, 4)


def on_device(grad_out, features, weight, edge_blocks, block_index, block_count, node_perm):
    block_side = edge_blocks.shape[1]
    stacked, table = regroup(node_perm, grad_out, block_index.T, block_count, SIZES)
    stacked = stacked.reshape(-1, block_side, grad_out.shape[1])
    nodes = grad_out.shape[0] * lax.axis_size("dom") * lax.axis_size("rep")
    grad_input, aggregated = slots(table, stacked, edge_blocks, weight)
    return (grad_input, reduce_parts(1.0 / math.sqrt(nodes), aggregated, features, SIZES))


def solution(mesh):
    in_specs = (
        P(("dom", "rep"), None),
        P(("dom", "rep"), None),
        P(),
        P(("dom", "rep"), None, None),
        P(("dom", "rep"), None),
        P(("dom", "rep")),
        P(("dom", "rep")),
    )
    out_specs = (P(("dom", "rep"), None), P("dom", "rep"))
    return jax.shard_map(
        on_device, mesh=mesh, in_specs=in_specs, out_specs=out_specs, check_vma=False
    )
```

```python
import math

import jax
import jax.numpy as jnp
from jax import lax
from jax.experimental import pallas as pl
from jax.experimental.pallas import tpu as pltpu
from jax.sharding import PartitionSpec as P

MESH = pl.DeviceIdType.MESH
SIZES = (8, 4, 4)


def wrap(value, size):
    return lax.rem(value + 2 * size, size)


def make_table(index, live):
    count = index.shape[1]
    here = lax.broadcasted_iota(jnp.int32, (count, count), 0).astype(jnp.float32)
    lane = lax.broadcasted_iota(jnp.int32, (count, count), 1)
    pair = jnp.broadcast_to(index[0:1, :] * 8 + index[1:2, :], (count, count))
    across = jnp.where(lane < live, pair, 4 * count).astype(jnp.float32)
    lane = lane.astype(jnp.float32)
    key = across.T

    def total(mask, value=1.0):
        return jnp.sum(jnp.where(mask, value, 0.0), axis=0, keepdims=True)

    ahead = (across < key) | ((across == key) & (lane < here))
    rank = jnp.sum(jnp.where(ahead, 1.0, 0.0), axis=1, keepdims=True)
    slot = total(rank == lane, here)
    now = total(rank == lane, key)
    before = total(rank == lane - 1.0, key)
    same = jnp.where((now == before) & (lane[0:1] > 0.0), 1.0, 0.0)
    rows = [slot, same]
    for part in range(4):
        wanted = lane + float(part * count)
        found = total(key <= wanted) - 1.0
        rows.append(jnp.where(total(key == wanted) > 0.0, found, float(count)))
    rows.append(jnp.zeros((2, count), jnp.float32))
    return jnp.concatenate(rows, axis=0).astype(jnp.int32)


def layer_kernel(
        zs_n, xs_n, ys_n, scale,
        perm_hbm, grad_hbm, index_hbm, count_ref, edge_hbm, feat_hbm, weight_hbm,
        gi_ref, out_ref,
        perm_ref, grad_ref, index_ref, edge_ref, feat_ref, weight_ref, ordered, raw, unperm,
        table_ref, tab, running, summed, dense, chunk, acc, agg_ref,
        part_other, part_mine, pair_in, sums, far_in, y_in, cols_sum, packed, dom_in,
        load_sem, own_sem, tab_sem, a_send, a_recv, y_send, y_recv, f_send, f_recv, p_send, p_recv,
        c_send, c_recv, s_send, s_recv, h_send, h_recv, d_send, d_recv):
    d = lax.axis_index("dom")
    r = lax.axis_index("rep")
    z, x = d // xs_n, lax.rem(d, xs_n)
    y, c = r // 2, lax.rem(r, 2)
    peers = zs_n * xs_n
    slot_rows = 4
    piece = 2 * ys_n * slot_rows
    side = edge_ref.shape[1]
    r_up = wrap(y + 1, ys_n) * 2 + c
    r_down = wrap(y - 1, ys_n) * 2 + c
    r_far = wrap(y + 2, ys_n) * 2 + c
    r_pair = r + 1 - 2 * c
    r_way = (r_up, r_down)
    group = peers // 2
    home = d // group
    bf16, f32 = jnp.bfloat16, jnp.float32

    def offset(j):
        return ((j + 1) // 2) * (2 * lax.rem(j, 2) - 1)

    loads = [pltpu.make_async_copy(a, b, load_sem.at[n]) for n, (a, b) in enumerate((
        (perm_hbm, perm_ref), (grad_hbm, grad_ref), (index_hbm, index_ref),
        (edge_hbm, edge_ref), (feat_hbm, feat_ref), (weight_hbm, weight_ref)))]
    for load in loads:
        load.start()

    barrier = pltpu.get_barrier_semaphore()

    @pl.loop(1, peers)
    def _(n):
        pl.semaphore_signal(barrier, inc=1, device_id={"dom": wrap(d + n, peers), "rep": r},
                            device_id_type=MESH)

    for other in (*r_way, r_pair):
        pl.semaphore_signal(barrier, inc=1, device_id={"dom": d, "rep": other},
                            device_id_type=MESH)

    @pl.when(c != home)
    def _():
        @pl.loop(0, peers)
        def _(n):
            pl.semaphore_signal(barrier, inc=1,
                                device_id={"dom": wrap(d + n, peers), "rep": r_pair},
                                device_id_type=MESH)

    loads[0].wait()
    perm = perm_ref[...]
    target = (perm // grad_ref.shape[0]) * slot_rows + lax.rem(perm, slot_rows)
    tile = 256
    loads[1].wait()

    @pl.loop(0, grad_ref.shape[0] // tile)
    def _(t):
        rows = lax.broadcasted_iota(jnp.int32, (tile, grad_ref.shape[0]), 0) + t * tile
        hot = jnp.where(rows == target, 1.0, 0.0).astype(bf16)
        ordered[pl.ds(pl.multiple_of(t * tile, tile), tile), :] = lax.dot_general(
            hot, grad_ref[...], (((1,), (0,)), ((), ())), preferred_element_type=f32).astype(bf16)

    loads[2].wait()
    table_ref[...] = make_table(index_ref[...], count_ref[0])
    tab_copy = pltpu.make_async_copy(table_ref, tab, tab_sem)
    tab_copy.start()
    q = lax.broadcasted_iota(jnp.int32, (tile, tile), 0)
    p = lax.broadcasted_iota(jnp.int32, (tile, tile), 1)
    wanted = lax.rem(q // slot_rows, 8) * piece + (q // piece) * slot_rows + lax.rem(q, slot_rows)
    unperm[...] = jnp.where(p == wanted, 1.0, 0.0).astype(bf16)

    pl.semaphore_wait(barrier, peers - 1 + 3 + group)

    own = pltpu.make_async_copy(
        ordered.at[pl.ds(pl.multiple_of(d * piece, piece), piece)], raw.at[z, x, r], own_sem)
    own.start()

    def a_copy(n, zs, xs):
        j, i = n // xs_n, lax.rem(n, xs_n)
        to = wrap(z + offset(j), zs_n) * xs_n + wrap(x + i, xs_n)
        return pltpu.make_async_remote_copy(
            src_ref=ordered.at[pl.ds(pl.multiple_of(to * piece, piece), piece)],
            dst_ref=raw.at[zs, xs, r],
            send_sem=a_send.at[n], recv_sem=a_recv.at[n],
            device_id={"dom": to, "rep": r}, device_id_type=MESH)

    @pl.loop(1, peers)
    def _(n):
        a_copy(n, z, x).start()

    def chunk_of(j):
        return wrap(z - offset(j), zs_n)

    def y_copy(j, way, owner):
        part = raw.at[chunk_of(j), :, owner]
        return pltpu.make_async_remote_copy(
            src_ref=part, dst_ref=part, send_sem=y_send.at[way, j], recv_sem=y_recv.at[way, j],
            device_id={"dom": d, "rep": r_way[way]}, device_id_type=MESH)

    half = xs_n // 2

    def f_copy(j, way, owner):
        part = raw.at[chunk_of(j), pl.ds(way * half, half), owner]
        return pltpu.make_async_remote_copy(
            src_ref=part, dst_ref=part, send_sem=f_send.at[way, j], recv_sem=f_recv.at[way, j],
            device_id={"dom": d, "rep": r_way[way]}, device_id_type=MESH)

    def p_copy(j, which, owner):
        part = raw.at[chunk_of(j), :, owner]
        return pltpu.make_async_remote_copy(
            src_ref=part, dst_ref=part, send_sem=p_send.at[which, j],
            recv_sem=p_recv.at[which, j],
            device_id={"dom": d, "rep": r_pair}, device_id_type=MESH)

    quarter = edge_ref.shape[0] // 4

    def sum_pairs(part):
        @pl.loop(0, quarter)
        def _(n):
            at = part * quarter + n
            slot = jnp.clip(tab[0, at], 0, edge_ref.shape[0] - 1)
            total = jnp.where(tab[1, at] > 0, running[...], 0.0) + edge_ref[slot].astype(f32)
            running[...] = total
            summed[at] = total.T.astype(bf16)

    loads[3].wait()
    tab_copy.wait()
    running[...] = jnp.zeros_like(running)
    summed[edge_ref.shape[0]] = jnp.zeros((side, side), bf16)
    sum_pairs(0)
    acc[...] = jnp.zeros_like(acc)

    @pl.loop(0, zs_n + 3)
    def _(step):
        @pl.when(step < zs_n)
        def _():
            j = step

            @pl.when(j == 0)
            def _():
                own.wait()

            @pl.loop(0, xs_n)
            def _(i):
                @pl.when(j * xs_n + i > 0)
                def _():
                    a_copy(j * xs_n + i, chunk_of(j), wrap(x - i, xs_n)).wait_recv()

            y_copy(j, 0, r).start()
            y_copy(j, 1, r).start()
            p_copy(j, 0, r).start()

        @pl.when((step >= 1) & (step < zs_n + 1))
        def _():
            j = step - 1
            y_copy(j, 0, r_down).wait_recv()
            f_copy(j, 0, r_down).start()
            p_copy(j, 1, r_down).start()
            y_copy(j, 1, r_up).wait_recv()
            f_copy(j, 1, r_up).start()
            p_copy(j, 2, r_up).start()

        @pl.when((step >= 2) & (step < zs_n + 2))
        def _():
            j = step - 2
            f_copy(j, 0, r_far).wait_recv()
            f_copy(j, 1, r_far).wait_recv()
            p_copy(j, 3, r_far).start()

        @pl.when(step < 3)
        def _():
            sum_pairs(step + 1)

        @pl.when(step >= 3)
        def _():
            j = step - 3
            zs = chunk_of(j)
            for t in range(8):
                for col in range(8):
                    pair = t * 64 + zs * 8 + col
                    place = tab[2 + pair // side, lax.rem(pair, side)]
                    dense[col * side:(col + 1) * side, t * side:(t + 1) * side] = summed[
                        jnp.clip(place, 0, edge_ref.shape[0])]
            flip = 1 - 2 * c
            p_copy(j, 0, r + flip).wait_recv()
            p_copy(j, 1, r_down + flip).wait_recv()
            p_copy(j, 2, r_up + flip).wait_recv()
            p_copy(j, 3, r_far + flip).wait_recv()
            for xs in range(xs_n):
                rows = raw[zs, xs].reshape(tile, acc.shape[1])
                placed = lax.dot_general(
                    unperm[...], rows, (((1,), (0,)), ((), ())),
                    preferred_element_type=f32).astype(bf16)
                for t in range(2 * ys_n):
                    chunk[t * side + xs * piece:t * side + (xs + 1) * piece, :] = placed[
                        t * piece:(t + 1) * piece, :]
            acc[...] += lax.dot_general(
                dense[...], chunk[...], (((1,), (0,)), ((), ())), preferred_element_type=f32)

    agg_ref[...] = acc[...].astype(bf16)
    for load in loads[4:]:
        load.wait()
    out_rows = out_ref.shape[0]
    tall, lanes = cols_sum.shape
    mid = tall // 2

    def partial(half):
        cols = feat_ref[:, pl.ds(pl.multiple_of(half * tall, tall), tall)]
        return lax.dot_general(
            cols, agg_ref[...], (((0,), (0,)), ((), ())),
            preferred_element_type=jnp.float32) * scale

    part_other[...] = partial(1 - c)

    def wide(n):
        return pl.ds(pl.multiple_of(wrap(y + n, ys_n) * lanes, lanes), lanes)

    def c_copy(n):
        return pltpu.make_async_remote_copy(
            src_ref=part_other.at[:, wide(n)], dst_ref=pair_in.at[n],
            send_sem=c_send.at[n], recv_sem=c_recv.at[n],
            device_id={"dom": d, "rep": r_pair}, device_id_type=MESH)

    def s_copy(way):
        return pltpu.make_async_remote_copy(
            src_ref=sums.at[2, pl.ds(way * mid, mid)], dst_ref=far_in.at[way],
            send_sem=s_send.at[way], recv_sem=s_recv.at[way],
            device_id={"dom": d, "rep": r_way[way]}, device_id_type=MESH)

    def h_copy(way, part):
        place = pl.ds(part * mid, mid)
        return pltpu.make_async_remote_copy(
            src_ref=sums.at[1 + 2 * way, place], dst_ref=y_in.at[way, place],
            send_sem=h_send.at[way, part], recv_sem=h_recv.at[way, part],
            device_id={"dom": d, "rep": r_way[way]}, device_id_type=MESH)

    def add_pair(n):
        c_copy(n).wait_recv()
        sums[n] = part_mine[:, wide(n)] + pair_in[n]

    for n in (2, 1, 3, 0):
        c_copy(n).start()
    part_mine[...] = partial(c)
    add_pair(2)
    for way in range(2):
        s_copy(way).start()
    for way in range(2):
        add_pair(1 + 2 * way)
        h_copy(way, 1 - way).start()
    add_pair(0)
    for way in range(2):
        s_copy(way).wait_recv()
        sums[1 + 2 * way, way * mid:(way + 1) * mid] += far_in[way]
        h_copy(way, way).start()
    for way in range(2):
        h_copy(way, 1 - way).wait_recv()
    for way in range(2):
        h_copy(way, way).wait_recv()
    cols_sum[...] = sums[0] + (y_in[0] + y_in[1])
    both = cols_sum[...].reshape(group, out_rows, lanes)
    low, high = both[:, :out_rows // 2], both[:, out_rows // 2:]
    left = lax.broadcasted_iota(jnp.int32, low.shape, 2) < lanes // 2
    packed[0] = jnp.where(left, low, pltpu.roll(high, lanes // 2, 2))
    packed[1] = jnp.where(left, pltpu.roll(low, lanes // 2, 2), high)

    def d_copy(n, core):
        return pltpu.make_async_remote_copy(
            src_ref=packed.at[core, n], dst_ref=dom_in.at[d],
            send_sem=d_send.at[core, n], recv_sem=d_recv.at[d],
            device_id={"dom": c * group + n, "rep": y * 2 + core}, device_id_type=MESH)

    @pl.loop(0, group)
    def _(m):
        n = lax.rem(m + d + group // 2, group)
        for core in range(2):
            @pl.when((c * group + n != d) | (c != core))
            def _():
                d_copy(n, core).start()

    gi_ref[...] = lax.dot_general(
        agg_ref[...], weight_ref[...], (((1,), (1,)), ((), ())),
        preferred_element_type=f32).astype(gi_ref.dtype)

    @pl.when(c == home)
    def _():
        dom_in[d] = packed[c, d - c * group]

    @pl.loop(0, peers)
    def _(s):
        @pl.when((s != d) | (c != home))
        def _():
            pltpu.make_async_remote_copy(
                src_ref=packed.at[0, 0], dst_ref=dom_in.at[s],
                send_sem=d_send.at[0, 0], recv_sem=d_recv.at[s],
                device_id={"dom": d, "rep": r_pair}, device_id_type=MESH).wait_recv()

    sums_of = [dom_in[s] for s in range(peers)]
    while len(sums_of) > 1:
        sums_of = [a + b for a, b in zip(sums_of[::2], sums_of[1::2])]
    total = sums_of[0]
    out_ref[:out_rows // 2] = total[:, :lanes // 2]
    out_ref[out_rows // 2:] = total[:, lanes // 2:]

    for n in range(ys_n):
        c_copy(n).wait_send()
    for way in range(2):
        s_copy(way).wait_send()
        for part in range(2):
            h_copy(way, part).wait_send()
    @pl.loop(0, group)
    def _(n):
        for core in range(2):
            @pl.when((c * group + n != d) | (c != core))
            def _():
                d_copy(n, core).wait_send()

    @pl.loop(1, peers)
    def _(n):
        a_copy(n, z, x).wait_send()

    @pl.loop(0, zs_n)
    def _(j):
        for way in range(2):
            y_copy(j, way, r).wait_send()
            f_copy(j, way, r).wait_send()
        for which in range(4):
            p_copy(j, which, r).wait_send()


def layer(perm, grad, index, count, edge, feat, weight, scale):
    zs_n, xs_n, ys_n = SIZES
    rows, width = grad.shape
    fin = feat.shape[1]
    reps, doms = 2 * ys_n, zs_n * xs_n
    piece = rows // doms
    slots, side = edge.shape[0], edge.shape[1]
    tall, lanes = fin // 2, width // ys_n
    out_rows = fin // doms
    far = pl.BlockSpec(memory_space=pltpu.HBM)
    vmem = pl.BlockSpec(memory_space=pltpu.VMEM)
    dma = pltpu.SemaphoreType.DMA
    f32, bf16 = jnp.float32, grad.dtype
    args = (perm.reshape(1, rows), grad, index, count, edge, feat, weight)
    args = tuple(a if n == 3 else pltpu.with_memory_space_constraint(a, pltpu.HBM)
                 for n, a in enumerate(args))
    return pl.pallas_call(
        lambda *refs: layer_kernel(zs_n, xs_n, ys_n, scale, *refs),
        out_shape=(jax.ShapeDtypeStruct((rows, fin), bf16),
                   jax.ShapeDtypeStruct((out_rows, lanes // 2), f32)),
        in_specs=[far] * 3 + [pl.BlockSpec(memory_space=pltpu.SMEM)] + [far] * 3,
        out_specs=(vmem, vmem),
        scratch_shapes=[
            pltpu.VMEM((1, rows), jnp.int32),
            pltpu.VMEM(grad.shape, bf16),
            pltpu.VMEM(index.shape, jnp.int32),
            pltpu.VMEM(edge.shape, bf16),
            pltpu.VMEM(feat.shape, bf16),
            pltpu.VMEM(weight.shape, bf16),
            pltpu.VMEM((rows, width), bf16),
            pltpu.VMEM((zs_n, xs_n, reps, piece, width), bf16),
            pltpu.VMEM((256, 256), bf16),
            pltpu.VMEM((8, slots), jnp.int32),
            pltpu.SMEM((8, slots), jnp.int32),
            pltpu.VMEM((side, side), f32),
            pltpu.VMEM((slots + 1, side, side), bf16),
            pltpu.VMEM((rows, rows), bf16),
            pltpu.VMEM((rows, width), bf16),
            pltpu.VMEM((rows, width), f32),
            pltpu.VMEM((rows, width), bf16),
            pltpu.VMEM((tall, width), f32), pltpu.VMEM((tall, width), f32),
            pltpu.VMEM((ys_n, tall, lanes), f32), pltpu.VMEM((ys_n, tall, lanes), f32),
            pltpu.VMEM((2, tall // 2, lanes), f32), pltpu.VMEM((2, tall, lanes), f32),
            pltpu.VMEM((tall, lanes), f32),
            pltpu.VMEM((2, doms // 2, out_rows // 2, lanes), f32),
            pltpu.VMEM((doms, out_rows // 2, lanes), f32),
            dma((6,)), dma, dma, dma((doms,)), dma((doms,)),
            dma((2, zs_n)), dma((2, zs_n)), dma((2, zs_n)), dma((2, zs_n)),
            dma((4, zs_n)), dma((4, zs_n)),
            dma((ys_n,)), dma((ys_n,)), dma((2,)), dma((2,)), dma((2, 2)), dma((2, 2)),
            dma((2, doms // 2)), dma((doms,)),
        ],
        compiler_params=pltpu.CompilerParams(
            collective_id=0, has_side_effects=True, vmem_limit_bytes=56 << 20),
        name="layer",
    )(*args)


def on_device(grad_out, features, weight, edge_blocks, block_index, block_count, node_perm):
    nodes = grad_out.shape[0] * lax.axis_size("dom") * lax.axis_size("rep")
    return layer(node_perm, grad_out, block_index.T, block_count, edge_blocks, features, weight,
                 1.0 / math.sqrt(nodes))


def solution(mesh):
    in_specs = (
        P(("dom", "rep"), None),
        P(("dom", "rep"), None),
        P(),
        P(("dom", "rep"), None, None),
        P(("dom", "rep"), None),
        P(("dom", "rep")),
        P(("dom", "rep")),
    )
    out_specs = (P(("dom", "rep"), None), P("dom", "rep"))
    return jax.shard_map(
        on_device, mesh=mesh, in_specs=in_specs, out_specs=out_specs, check_vma=False
    )
```

```python
import math

import jax
import jax.numpy as jnp
from jax import lax
from jax.experimental import pallas as pl
from jax.experimental.pallas import tpu as pltpu
from jax.sharding import PartitionSpec as P

MESH = pl.DeviceIdType.MESH
SIZES = (8, 4, 4)


def wrap(value, size):
    return lax.rem(value + 2 * size, size)


def make_table(index, live):
    count = index.shape[1]
    here = lax.broadcasted_iota(jnp.int32, (count, count), 0).astype(jnp.float32)
    lane = lax.broadcasted_iota(jnp.int32, (count, count), 1)
    pair = jnp.broadcast_to(index[0:1, :] * 8 + index[1:2, :], (count, count))
    across = jnp.where(lane < live, pair, 4 * count).astype(jnp.float32)
    lane = lane.astype(jnp.float32)
    key = across.T

    def total(mask, value=1.0):
        return jnp.sum(jnp.where(mask, value, 0.0), axis=0, keepdims=True)

    ahead = (across < key) | ((across == key) & (lane < here))
    rank = jnp.sum(jnp.where(ahead, 1.0, 0.0), axis=1, keepdims=True)
    slot = total(rank == lane, here)
    now = total(rank == lane, key)
    before = total(rank == lane - 1.0, key)
    same = jnp.where((now == before) & (lane[0:1] > 0.0), 1.0, 0.0)
    rows = [slot, same]
    for part in range(4):
        wanted = lane + float(part * count)
        found = total(key <= wanted) - 1.0
        rows.append(jnp.where(total(key == wanted) > 0.0, found, float(count)))
    rows.append(jnp.zeros((2, count), jnp.float32))
    return jnp.concatenate(rows, axis=0).astype(jnp.int32)


def layer_kernel(
        zs_n, xs_n, ys_n, scale,
        perm_hbm, grad_hbm, index_hbm, count_ref, edge_hbm, feat_hbm,
        agg_ref, out_ref,
        perm_ref, grad_ref, index_ref, edge_ref, feat_ref, ordered, raw, unperm,
        table_ref, tab, running, summed, dense, chunk, acc,
        part_other, part_mine, pair_in, sums, far_in, y_in, cols_sum, packed, dom_in,
        load_sem, own_sem, tab_sem, a_send, a_recv, y_send, y_recv, f_send, f_recv, p_send, p_recv,
        c_send, c_recv, s_send, s_recv, h_send, h_recv, d_send, d_recv):
    d = lax.axis_index("dom")
    r = lax.axis_index("rep")
    z, x = d // xs_n, lax.rem(d, xs_n)
    y, c = r // 2, lax.rem(r, 2)
    peers = zs_n * xs_n
    slot_rows = 4
    piece = 2 * ys_n * slot_rows
    side = edge_ref.shape[1]
    r_up = wrap(y + 1, ys_n) * 2 + c
    r_down = wrap(y - 1, ys_n) * 2 + c
    r_far = wrap(y + 2, ys_n) * 2 + c
    r_pair = r + 1 - 2 * c
    r_way = (r_up, r_down)
    group = peers // 2
    home = d // group
    bf16, f32 = jnp.bfloat16, jnp.float32

    def offset(j):
        return ((j + 1) // 2) * (2 * lax.rem(j, 2) - 1)

    loads = [pltpu.make_async_copy(a, b, load_sem.at[n]) for n, (a, b) in enumerate((
        (perm_hbm, perm_ref), (grad_hbm, grad_ref), (index_hbm, index_ref),
        (edge_hbm, edge_ref), (feat_hbm, feat_ref)))]
    for load in loads[:3]:
        load.start()

    barrier = pltpu.get_barrier_semaphore()

    @pl.loop(1, peers)
    def _(n):
        pl.semaphore_signal(barrier, inc=1, device_id={"dom": wrap(d + n, peers), "rep": r},
                            device_id_type=MESH)

    for other in (*r_way, r_pair):
        pl.semaphore_signal(barrier, inc=1, device_id={"dom": d, "rep": other},
                            device_id_type=MESH)

    @pl.when(c != home)
    def _():
        @pl.loop(0, peers)
        def _(n):
            pl.semaphore_signal(barrier, inc=1,
                                device_id={"dom": wrap(d + n, peers), "rep": r_pair},
                                device_id_type=MESH)

    loads[0].wait()
    perm = perm_ref[...]
    target = (perm // grad_ref.shape[0]) * slot_rows + lax.rem(perm, slot_rows)
    tile = 256
    loads[1].wait()
    for load in loads[3:]:
        load.start()

    @pl.loop(0, grad_ref.shape[0] // tile)
    def _(t):
        rows = lax.broadcasted_iota(jnp.int32, (tile, grad_ref.shape[0]), 0) + t * tile
        hot = jnp.where(rows == target, 1.0, 0.0).astype(bf16)
        ordered[pl.ds(pl.multiple_of(t * tile, tile), tile), :] = lax.dot_general(
            hot, grad_ref[...], (((1,), (0,)), ((), ())), preferred_element_type=f32).astype(bf16)

    loads[2].wait()
    table_ref[...] = make_table(index_ref[...], count_ref[0])
    tab_copy = pltpu.make_async_copy(table_ref, tab, tab_sem)
    tab_copy.start()
    q = lax.broadcasted_iota(jnp.int32, (tile, tile), 0)
    p = lax.broadcasted_iota(jnp.int32, (tile, tile), 1)
    wanted = lax.rem(q // slot_rows, 8) * piece + (q // piece) * slot_rows + lax.rem(q, slot_rows)
    unperm[...] = jnp.where(p == wanted, 1.0, 0.0).astype(bf16)

    pl.semaphore_wait(barrier, peers - 1 + 3 + group)

    own = pltpu.make_async_copy(
        ordered.at[pl.ds(pl.multiple_of(d * piece, piece), piece)], raw.at[z, x, r], own_sem)
    own.start()

    def a_copy(n, zs, xs):
        j, i = n // xs_n, lax.rem(n, xs_n)
        to = wrap(z + offset(j), zs_n) * xs_n + wrap(x + i, xs_n)
        return pltpu.make_async_remote_copy(
            src_ref=ordered.at[pl.ds(pl.multiple_of(to * piece, piece), piece)],
            dst_ref=raw.at[zs, xs, r],
            send_sem=a_send.at[n], recv_sem=a_recv.at[n],
            device_id={"dom": to, "rep": r}, device_id_type=MESH)

    @pl.loop(1, peers)
    def _(n):
        a_copy(n, z, x).start()

    def chunk_of(j):
        return wrap(z - offset(j), zs_n)

    def y_copy(j, way, owner):
        part = raw.at[chunk_of(j), :, owner]
        return pltpu.make_async_remote_copy(
            src_ref=part, dst_ref=part, send_sem=y_send.at[way, j], recv_sem=y_recv.at[way, j],
            device_id={"dom": d, "rep": r_way[way]}, device_id_type=MESH)

    half = xs_n // 2

    def f_copy(j, way, owner):
        part = raw.at[chunk_of(j), pl.ds(way * half, half), owner]
        return pltpu.make_async_remote_copy(
            src_ref=part, dst_ref=part, send_sem=f_send.at[way, j], recv_sem=f_recv.at[way, j],
            device_id={"dom": d, "rep": r_way[way]}, device_id_type=MESH)

    def p_copy(j, which, owner):
        part = raw.at[chunk_of(j), :, owner]
        return pltpu.make_async_remote_copy(
            src_ref=part, dst_ref=part, send_sem=p_send.at[which, j],
            recv_sem=p_recv.at[which, j],
            device_id={"dom": d, "rep": r_pair}, device_id_type=MESH)

    quarter = edge_ref.shape[0] // 4

    def sum_pairs(part):
        @pl.loop(0, quarter)
        def _(n):
            at = part * quarter + n
            slot = jnp.clip(tab[0, at], 0, edge_ref.shape[0] - 1)
            total = jnp.where(tab[1, at] > 0, running[...], 0.0) + edge_ref[slot].astype(f32)
            running[...] = total
            summed[at] = total.T.astype(bf16)

    def send_own(j):
        @pl.loop(0, xs_n)
        def _(i):
            @pl.when(j * xs_n + i > 0)
            def _():
                a_copy(j * xs_n + i, chunk_of(j), wrap(x - i, xs_n)).wait_recv()

        y_copy(j, 0, r).start()
        y_copy(j, 1, r).start()
        p_copy(j, 0, r).start()

    own.wait()
    send_own(0)
    loads[3].wait()
    tab_copy.wait()
    running[...] = jnp.zeros_like(running)
    summed[edge_ref.shape[0]] = jnp.zeros((side, side), bf16)
    sum_pairs(0)
    acc[...] = jnp.zeros_like(acc)

    @pl.loop(0, zs_n + 3)
    def _(step):
        @pl.when(step + 1 < zs_n)
        def _():
            send_own(step + 1)

        @pl.when((step >= 1) & (step < zs_n + 1))
        def _():
            j = step - 1
            y_copy(j, 0, r_down).wait_recv()
            f_copy(j, 0, r_down).start()
            p_copy(j, 1, r_down).start()
            y_copy(j, 1, r_up).wait_recv()
            f_copy(j, 1, r_up).start()
            p_copy(j, 2, r_up).start()

        @pl.when((step >= 2) & (step < zs_n + 2))
        def _():
            j = step - 2
            f_copy(j, 0, r_far).wait_recv()
            f_copy(j, 1, r_far).wait_recv()
            p_copy(j, 3, r_far).start()

        @pl.when(step < 3)
        def _():
            sum_pairs(step + 1)

        @pl.when(step >= 3)
        def _():
            j = step - 3
            zs = chunk_of(j)
            for t in range(8):
                for col in range(8):
                    pair = t * 64 + zs * 8 + col
                    place = tab[2 + pair // side, lax.rem(pair, side)]
                    dense[col * side:(col + 1) * side, t * side:(t + 1) * side] = summed[
                        jnp.clip(place, 0, edge_ref.shape[0])]
            flip = 1 - 2 * c
            p_copy(j, 0, r + flip).wait_recv()
            p_copy(j, 1, r_down + flip).wait_recv()
            p_copy(j, 2, r_up + flip).wait_recv()
            p_copy(j, 3, r_far + flip).wait_recv()
            for xs in range(xs_n):
                rows = raw[zs, xs].reshape(tile, acc.shape[1])
                placed = lax.dot_general(
                    unperm[...], rows, (((1,), (0,)), ((), ())),
                    preferred_element_type=f32).astype(bf16)
                for t in range(2 * ys_n):
                    chunk[t * side + xs * piece:t * side + (xs + 1) * piece, :] = placed[
                        t * piece:(t + 1) * piece, :]
            acc[...] += lax.dot_general(
                dense[...], chunk[...], (((1,), (0,)), ((), ())), preferred_element_type=f32)

    agg_ref[...] = acc[...].astype(bf16)
    for load in loads[4:]:
        load.wait()
    out_rows = out_ref.shape[0]
    tall, lanes = cols_sum.shape
    mid = tall // 2

    def partial(half):
        cols = feat_ref[:, pl.ds(pl.multiple_of(half * tall, tall), tall)]
        return lax.dot_general(
            cols, agg_ref[...], (((0,), (0,)), ((), ())),
            preferred_element_type=jnp.float32) * scale

    part_other[...] = partial(1 - c)

    def wide(n):
        return pl.ds(pl.multiple_of(wrap(y + n, ys_n) * lanes, lanes), lanes)

    def c_copy(n):
        return pltpu.make_async_remote_copy(
            src_ref=part_other.at[:, wide(n)], dst_ref=pair_in.at[n],
            send_sem=c_send.at[n], recv_sem=c_recv.at[n],
            device_id={"dom": d, "rep": r_pair}, device_id_type=MESH)

    def s_copy(way):
        return pltpu.make_async_remote_copy(
            src_ref=sums.at[2, pl.ds(way * mid, mid)], dst_ref=far_in.at[way],
            send_sem=s_send.at[way], recv_sem=s_recv.at[way],
            device_id={"dom": d, "rep": r_way[way]}, device_id_type=MESH)

    def h_copy(way, part):
        place = pl.ds(part * mid, mid)
        return pltpu.make_async_remote_copy(
            src_ref=sums.at[1 + 2 * way, place], dst_ref=y_in.at[way, place],
            send_sem=h_send.at[way, part], recv_sem=h_recv.at[way, part],
            device_id={"dom": d, "rep": r_way[way]}, device_id_type=MESH)

    def add_pair(n):
        c_copy(n).wait_recv()
        sums[n] = part_mine[:, wide(n)] + pair_in[n]

    for n in (2, 1, 3, 0):
        c_copy(n).start()
    part_mine[...] = partial(c)
    add_pair(2)
    for way in range(2):
        s_copy(way).start()
    for way in range(2):
        add_pair(1 + 2 * way)
        h_copy(way, 1 - way).start()
    add_pair(0)
    for way in range(2):
        s_copy(way).wait_recv()
        sums[1 + 2 * way, way * mid:(way + 1) * mid] += far_in[way]
        h_copy(way, way).start()
    for way in range(2):
        h_copy(way, 1 - way).wait_recv()
    for way in range(2):
        h_copy(way, way).wait_recv()
    cols_sum[...] = sums[0] + (y_in[0] + y_in[1])
    both = cols_sum[...].reshape(group, out_rows, lanes)
    low, high = both[:, :out_rows // 2], both[:, out_rows // 2:]
    left = lax.broadcasted_iota(jnp.int32, low.shape, 2) < lanes // 2
    packed[0] = jnp.where(left, low, pltpu.roll(high, lanes // 2, 2))
    packed[1] = jnp.where(left, pltpu.roll(low, lanes // 2, 2), high)

    def d_copy(n, core):
        return pltpu.make_async_remote_copy(
            src_ref=packed.at[core, n], dst_ref=dom_in.at[d],
            send_sem=d_send.at[core, n], recv_sem=d_recv.at[d],
            device_id={"dom": c * group + n, "rep": y * 2 + core}, device_id_type=MESH)

    @pl.loop(0, group)
    def _(m):
        n = lax.rem(m + d + group // 2, group)
        for core in range(2):
            @pl.when((c * group + n != d) | (c != core))
            def _():
                d_copy(n, core).start()

    @pl.when(c == home)
    def _():
        dom_in[d] = packed[c, d - c * group]

    @pl.loop(0, peers)
    def _(s):
        @pl.when((s != d) | (c != home))
        def _():
            pltpu.make_async_remote_copy(
                src_ref=packed.at[0, 0], dst_ref=dom_in.at[s],
                send_sem=d_send.at[0, 0], recv_sem=d_recv.at[s],
                device_id={"dom": d, "rep": r_pair}, device_id_type=MESH).wait_recv()

    sums_of = [dom_in[s] for s in range(peers)]
    while len(sums_of) > 1:
        sums_of = [a + b for a, b in zip(sums_of[::2], sums_of[1::2])]
    total = sums_of[0]
    out_ref[:out_rows // 2] = total[:, :lanes // 2]
    out_ref[out_rows // 2:] = total[:, lanes // 2:]

    for n in range(ys_n):
        c_copy(n).wait_send()
    for way in range(2):
        s_copy(way).wait_send()
        for part in range(2):
            h_copy(way, part).wait_send()
    @pl.loop(0, group)
    def _(n):
        for core in range(2):
            @pl.when((c * group + n != d) | (c != core))
            def _():
                d_copy(n, core).wait_send()

    @pl.loop(1, peers)
    def _(n):
        a_copy(n, z, x).wait_send()

    @pl.loop(0, zs_n)
    def _(j):
        for way in range(2):
            y_copy(j, way, r).wait_send()
            f_copy(j, way, r).wait_send()
        for which in range(4):
            p_copy(j, which, r).wait_send()


def layer(perm, grad, index, count, edge, feat, scale):
    zs_n, xs_n, ys_n = SIZES
    rows, width = grad.shape
    fin = feat.shape[1]
    reps, doms = 2 * ys_n, zs_n * xs_n
    piece = rows // doms
    slots, side = edge.shape[0], edge.shape[1]
    tall, lanes = fin // 2, width // ys_n
    out_rows = fin // doms
    far = pl.BlockSpec(memory_space=pltpu.HBM)
    vmem = pl.BlockSpec(memory_space=pltpu.VMEM)
    dma = pltpu.SemaphoreType.DMA
    f32, bf16 = jnp.float32, grad.dtype
    args = (perm.reshape(1, rows), grad, index, count, edge, feat)
    args = tuple(a if n == 3 else pltpu.with_memory_space_constraint(a, pltpu.HBM)
                 for n, a in enumerate(args))
    return pl.pallas_call(
        lambda *refs: layer_kernel(zs_n, xs_n, ys_n, scale, *refs),
        out_shape=(jax.ShapeDtypeStruct((rows, width), bf16),
                   jax.ShapeDtypeStruct((out_rows, lanes // 2), f32)),
        in_specs=[far] * 3 + [pl.BlockSpec(memory_space=pltpu.SMEM)] + [far] * 2,
        out_specs=(vmem, vmem),
        scratch_shapes=[
            pltpu.VMEM((1, rows), jnp.int32),
            pltpu.VMEM(grad.shape, bf16),
            pltpu.VMEM(index.shape, jnp.int32),
            pltpu.VMEM(edge.shape, bf16),
            pltpu.VMEM(feat.shape, bf16),
            pltpu.VMEM((rows, width), bf16),
            pltpu.VMEM((zs_n, xs_n, reps, piece, width), bf16),
            pltpu.VMEM((256, 256), bf16),
            pltpu.VMEM((8, slots), jnp.int32),
            pltpu.SMEM((8, slots), jnp.int32),
            pltpu.VMEM((side, side), f32),
            pltpu.VMEM((slots + 1, side, side), bf16),
            pltpu.VMEM((rows, rows), bf16),
            pltpu.VMEM((rows, width), bf16),
            pltpu.VMEM((rows, width), f32),
            pltpu.VMEM((tall, width), f32), pltpu.VMEM((tall, width), f32),
            pltpu.VMEM((ys_n, tall, lanes), f32), pltpu.VMEM((ys_n, tall, lanes), f32),
            pltpu.VMEM((2, tall // 2, lanes), f32), pltpu.VMEM((2, tall, lanes), f32),
            pltpu.VMEM((tall, lanes), f32),
            pltpu.VMEM((2, doms // 2, out_rows // 2, lanes), f32),
            pltpu.VMEM((doms, out_rows // 2, lanes), f32),
            dma((5,)), dma, dma, dma((doms,)), dma((doms,)),
            dma((2, zs_n)), dma((2, zs_n)), dma((2, zs_n)), dma((2, zs_n)),
            dma((4, zs_n)), dma((4, zs_n)),
            dma((ys_n,)), dma((ys_n,)), dma((2,)), dma((2,)), dma((2, 2)), dma((2, 2)),
            dma((2, doms // 2)), dma((doms,)),
        ],
        compiler_params=pltpu.CompilerParams(
            collective_id=0, has_side_effects=True, vmem_limit_bytes=48 << 20),
        name="layer",
    )(*args)


def finish_kernel(agg_ref, weight_ref, sum_ref, gi_ref, out_ref):
    gi_ref[...] = lax.dot_general(
        agg_ref[...], weight_ref[...], (((1,), (1,)), ((), ())),
        preferred_element_type=jnp.float32).astype(gi_ref.dtype)
    out_ref[...] = sum_ref[...]


def finish(agg, weight, summed):
    rows, width = agg.shape
    tile = 256
    whole = pl.BlockSpec(summed.shape, lambda i: (0, 0))
    return pl.pallas_call(
        finish_kernel,
        grid=(rows // tile,),
        out_shape=(jax.ShapeDtypeStruct((rows, weight.shape[0]), agg.dtype),
                   jax.ShapeDtypeStruct(summed.shape, summed.dtype)),
        in_specs=[pl.BlockSpec((tile, width), lambda i: (i, 0)),
                  pl.BlockSpec(weight.shape, lambda i: (0, 0)), whole],
        out_specs=(pl.BlockSpec((tile, weight.shape[0]), lambda i: (i, 0)), whole),
        compiler_params=pltpu.CompilerParams(vmem_limit_bytes=8 << 20),
        name="finish",
    )(agg, weight, summed)


def on_device(grad_out, features, weight, edge_blocks, block_index, block_count, node_perm):
    nodes = grad_out.shape[0] * lax.axis_size("dom") * lax.axis_size("rep")
    aggregated, summed = layer(
        node_perm, grad_out, block_index.T, block_count, edge_blocks, features,
        1.0 / math.sqrt(nodes))
    return finish(aggregated, weight, summed)


def solution(mesh):
    in_specs = (
        P(("dom", "rep"), None),
        P(("dom", "rep"), None),
        P(),
        P(("dom", "rep"), None, None),
        P(("dom", "rep"), None),
        P(("dom", "rep")),
        P(("dom", "rep")),
    )
    out_specs = (P(("dom", "rep"), None), P("dom", "rep"))
    return jax.shard_map(
        on_device, mesh=mesh, in_specs=in_specs, out_specs=out_specs, check_vma=False
    )
```

```python
import math

import jax
import jax.numpy as jnp
from jax import lax
from jax.experimental import pallas as pl
from jax.experimental.pallas import tpu as pltpu
from jax.sharding import PartitionSpec as P

MESH = pl.DeviceIdType.MESH
SIZES = (8, 4, 4)


def wrap(value, size):
    return lax.rem(value + 2 * size, size)


def make_table(index, live):
    count = index.shape[1]
    here = lax.broadcasted_iota(jnp.int32, (count, count), 0).astype(jnp.float32)
    lane = lax.broadcasted_iota(jnp.int32, (count, count), 1)
    pair = jnp.broadcast_to(index[0:1, :] * 8 + index[1:2, :], (count, count))
    across = jnp.where(lane < live, pair, 4 * count).astype(jnp.float32)
    lane = lane.astype(jnp.float32)
    key = across.T

    def total(mask, value=1.0):
        return jnp.sum(jnp.where(mask, value, 0.0), axis=0, keepdims=True)

    ahead = (across < key) | ((across == key) & (lane < here))
    rank = jnp.sum(jnp.where(ahead, 1.0, 0.0), axis=1, keepdims=True)
    slot = total(rank == lane, here)
    now = total(rank == lane, key)
    before = total(rank == lane - 1.0, key)
    same = jnp.where((now == before) & (lane[0:1] > 0.0), 1.0, 0.0)
    rows = [slot, same]
    for part in range(4):
        wanted = lane + float(part * count)
        found = total(key <= wanted) - 1.0
        rows.append(jnp.where(total(key == wanted) > 0.0, found, float(count)))
    rows.append(jnp.zeros((2, count), jnp.float32))
    return jnp.concatenate(rows, axis=0).astype(jnp.int32)


def layer_kernel(
        zs_n, xs_n, ys_n, scale,
        perm_hbm, grad_hbm, index_hbm, count_ref, edge_hbm, feat_hbm,
        weight_hbm, gi_ref, out_ref,
        perm_ref, grad_ref, index_ref, edge_ref, feat_ref, weight_ref, ordered, raw, unperm,
        table_ref, tab, running, summed, dense, chunk, acc, agg_ref,
        part_other, part_mine, pair_in, sums, far_in, y_in, cols_sum, packed, dom_in,
        load_sem, own_sem, tab_sem, a_send, a_recv, y_send, y_recv, f_send, f_recv, p_send, p_recv,
        c_send, c_recv, s_send, s_recv, h_send, h_recv, d_send, d_recv):
    d = lax.axis_index("dom")
    r = lax.axis_index("rep")
    z, x = d // xs_n, lax.rem(d, xs_n)
    y, c = r // 2, lax.rem(r, 2)
    peers = zs_n * xs_n
    slot_rows = 4
    piece = 2 * ys_n * slot_rows
    side = edge_ref.shape[1]
    r_up = wrap(y + 1, ys_n) * 2 + c
    r_down = wrap(y - 1, ys_n) * 2 + c
    r_far = wrap(y + 2, ys_n) * 2 + c
    r_pair = r + 1 - 2 * c
    r_way = (r_up, r_down)
    group = peers // 2
    home = d // group
    bf16, f32 = jnp.bfloat16, jnp.float32

    def offset(j):
        return ((j + 1) // 2) * (2 * lax.rem(j, 2) - 1)

    loads = [pltpu.make_async_copy(a, b, load_sem.at[n]) for n, (a, b) in enumerate((
        (perm_hbm, perm_ref), (grad_hbm, grad_ref), (index_hbm, index_ref),
        (edge_hbm, edge_ref), (feat_hbm, feat_ref), (weight_hbm, weight_ref)))]
    for load in loads[:3]:
        load.start()

    barrier = pltpu.get_barrier_semaphore()

    @pl.loop(1, peers)
    def _(n):
        pl.semaphore_signal(barrier, inc=1, device_id={"dom": wrap(d + n, peers), "rep": r},
                            device_id_type=MESH)

    for other in (*r_way, r_pair):
        pl.semaphore_signal(barrier, inc=1, device_id={"dom": d, "rep": other},
                            device_id_type=MESH)

    @pl.when(c != home)
    def _():
        @pl.loop(0, peers)
        def _(n):
            pl.semaphore_signal(barrier, inc=1,
                                device_id={"dom": wrap(d + n, peers), "rep": r_pair},
                                device_id_type=MESH)

    loads[0].wait()
    perm = perm_ref[...]
    target = (perm // grad_ref.shape[0]) * slot_rows + lax.rem(perm, slot_rows)
    tile = 256
    loads[1].wait()
    for load in loads[3:]:
        load.start()

    @pl.loop(0, grad_ref.shape[0] // tile)
    def _(t):
        rows = lax.broadcasted_iota(jnp.int32, (tile, grad_ref.shape[0]), 0) + t * tile
        hot = jnp.where(rows == target, 1.0, 0.0).astype(bf16)
        ordered[pl.ds(pl.multiple_of(t * tile, tile), tile), :] = lax.dot_general(
            hot, grad_ref[...], (((1,), (0,)), ((), ())), preferred_element_type=f32).astype(bf16)

    loads[2].wait()
    table_ref[...] = make_table(index_ref[...], count_ref[0])
    tab_copy = pltpu.make_async_copy(table_ref, tab, tab_sem)
    tab_copy.start()
    q = lax.broadcasted_iota(jnp.int32, (tile, tile), 0)
    p = lax.broadcasted_iota(jnp.int32, (tile, tile), 1)
    wanted = lax.rem(q // slot_rows, 8) * piece + (q // piece) * slot_rows + lax.rem(q, slot_rows)
    unperm[...] = jnp.where(p == wanted, 1.0, 0.0).astype(bf16)

    pl.semaphore_wait(barrier, peers - 1 + 3 + group)

    own = pltpu.make_async_copy(
        ordered.at[pl.ds(pl.multiple_of(d * piece, piece), piece)], raw.at[z, x, r], own_sem)
    own.start()

    def a_copy(n, zs, xs):
        j, i = n // xs_n, lax.rem(n, xs_n)
        to = wrap(z + offset(j), zs_n) * xs_n + wrap(x + i, xs_n)
        return pltpu.make_async_remote_copy(
            src_ref=ordered.at[pl.ds(pl.multiple_of(to * piece, piece), piece)],
            dst_ref=raw.at[zs, xs, r],
            send_sem=a_send.at[n], recv_sem=a_recv.at[n],
            device_id={"dom": to, "rep": r}, device_id_type=MESH)

    @pl.loop(1, peers)
    def _(n):
        a_copy(n, z, x).start()

    def chunk_of(j):
        return wrap(z - offset(j), zs_n)

    def y_copy(j, way, owner):
        part = raw.at[chunk_of(j), :, owner]
        return pltpu.make_async_remote_copy(
            src_ref=part, dst_ref=part, send_sem=y_send.at[way, j], recv_sem=y_recv.at[way, j],
            device_id={"dom": d, "rep": r_way[way]}, device_id_type=MESH)

    half = xs_n // 2

    def f_copy(j, way, owner):
        part = raw.at[chunk_of(j), pl.ds(way * half, half), owner]
        return pltpu.make_async_remote_copy(
            src_ref=part, dst_ref=part, send_sem=f_send.at[way, j], recv_sem=f_recv.at[way, j],
            device_id={"dom": d, "rep": r_way[way]}, device_id_type=MESH)

    def p_copy(j, which, owner):
        part = raw.at[chunk_of(j), :, owner]
        return pltpu.make_async_remote_copy(
            src_ref=part, dst_ref=part, send_sem=p_send.at[which, j],
            recv_sem=p_recv.at[which, j],
            device_id={"dom": d, "rep": r_pair}, device_id_type=MESH)

    quarter = edge_ref.shape[0] // 4

    def sum_pairs(part):
        @pl.loop(0, quarter)
        def _(n):
            at = part * quarter + n
            slot = jnp.clip(tab[0, at], 0, edge_ref.shape[0] - 1)
            total = jnp.where(tab[1, at] > 0, running[...], 0.0) + edge_ref[slot].astype(f32)
            running[...] = total
            summed[at] = total.T.astype(bf16)

    def send_own(j):
        @pl.loop(0, xs_n)
        def _(i):
            @pl.when(j * xs_n + i > 0)
            def _():
                a_copy(j * xs_n + i, chunk_of(j), wrap(x - i, xs_n)).wait_recv()

        y_copy(j, 0, r).start()
        y_copy(j, 1, r).start()
        p_copy(j, 0, r).start()

    own.wait()
    send_own(0)
    loads[3].wait()
    tab_copy.wait()
    running[...] = jnp.zeros_like(running)
    summed[edge_ref.shape[0]] = jnp.zeros((side, side), bf16)
    sum_pairs(0)
    acc[...] = jnp.zeros_like(acc)

    @pl.loop(0, zs_n + 3)
    def _(step):
        @pl.when(step + 1 < zs_n)
        def _():
            send_own(step + 1)

        @pl.when((step >= 1) & (step < zs_n + 1))
        def _():
            j = step - 1
            y_copy(j, 0, r_down).wait_recv()
            f_copy(j, 0, r_down).start()
            p_copy(j, 1, r_down).start()
            y_copy(j, 1, r_up).wait_recv()
            f_copy(j, 1, r_up).start()
            p_copy(j, 2, r_up).start()

        @pl.when(step < 3)
        def _():
            sum_pairs(step + 1)

        @pl.when(step >= 3)
        def _():
            j = step - 3
            zs = chunk_of(j)
            for t in range(8):
                for col in range(8):
                    pair = t * 64 + zs * 8 + col
                    place = tab[2 + pair // side, lax.rem(pair, side)]
                    dense[col * side:(col + 1) * side, t * side:(t + 1) * side] = summed[
                        jnp.clip(place, 0, edge_ref.shape[0])]
            flip = 1 - 2 * c
            p_copy(j, 0, r + flip).wait_recv()
            p_copy(j, 1, r_down + flip).wait_recv()
            p_copy(j, 2, r_up + flip).wait_recv()
            p_copy(j, 3, r_far + flip).wait_recv()
            for xs in range(xs_n):
                rows = raw[zs, xs].reshape(tile, acc.shape[1])
                placed = lax.dot_general(
                    unperm[...], rows, (((1,), (0,)), ((), ())),
                    preferred_element_type=f32).astype(bf16)
                for t in range(2 * ys_n):
                    chunk[t * side + xs * piece:t * side + (xs + 1) * piece, :] = placed[
                        t * piece:(t + 1) * piece, :]
            acc[...] += lax.dot_general(
                dense[...], chunk[...], (((1,), (0,)), ((), ())), preferred_element_type=f32)

        @pl.when((step >= 2) & (step < zs_n + 2))
        def _():
            j = step - 2
            f_copy(j, 0, r_far).wait_recv()
            f_copy(j, 1, r_far).wait_recv()
            p_copy(j, 3, r_far).start()

    agg_ref[...] = acc[...].astype(bf16)
    for load in loads[4:]:
        load.wait()
    out_rows = out_ref.shape[0]
    tall, lanes = cols_sum.shape
    mid = tall // 2

    def partial(half):
        cols = feat_ref[:, pl.ds(pl.multiple_of(half * tall, tall), tall)]
        return lax.dot_general(
            cols, agg_ref[...], (((0,), (0,)), ((), ())),
            preferred_element_type=jnp.float32) * scale

    part_other[...] = partial(1 - c)

    def wide(n):
        return pl.ds(pl.multiple_of(wrap(y + n, ys_n) * lanes, lanes), lanes)

    def c_copy(n):
        return pltpu.make_async_remote_copy(
            src_ref=part_other.at[:, wide(n)], dst_ref=pair_in.at[n],
            send_sem=c_send.at[n], recv_sem=c_recv.at[n],
            device_id={"dom": d, "rep": r_pair}, device_id_type=MESH)

    def s_copy(way):
        return pltpu.make_async_remote_copy(
            src_ref=sums.at[2, pl.ds(way * mid, mid)], dst_ref=far_in.at[way],
            send_sem=s_send.at[way], recv_sem=s_recv.at[way],
            device_id={"dom": d, "rep": r_way[way]}, device_id_type=MESH)

    def h_copy(way, part):
        place = pl.ds(part * mid, mid)
        return pltpu.make_async_remote_copy(
            src_ref=sums.at[1 + 2 * way, place], dst_ref=y_in.at[way, place],
            send_sem=h_send.at[way, part], recv_sem=h_recv.at[way, part],
            device_id={"dom": d, "rep": r_way[way]}, device_id_type=MESH)

    def add_pair(n):
        c_copy(n).wait_recv()
        sums[n] = part_mine[:, wide(n)] + pair_in[n]

    for n in (2, 1, 3, 0):
        c_copy(n).start()
    part_mine[...] = partial(c)
    add_pair(2)
    for way in range(2):
        s_copy(way).start()
    for way in range(2):
        add_pair(1 + 2 * way)
        h_copy(way, 1 - way).start()
    add_pair(0)
    for way in range(2):
        s_copy(way).wait_recv()
        sums[1 + 2 * way, way * mid:(way + 1) * mid] += far_in[way]
        h_copy(way, way).start()
    for way in range(2):
        h_copy(way, 1 - way).wait_recv()
    for way in range(2):
        h_copy(way, way).wait_recv()
    cols_sum[...] = sums[0] + (y_in[0] + y_in[1])
    both = cols_sum[...].reshape(group, out_rows, lanes)
    low, high = both[:, :out_rows // 2], both[:, out_rows // 2:]
    left = lax.broadcasted_iota(jnp.int32, low.shape, 2) < lanes // 2
    packed[0] = jnp.where(left, low, pltpu.roll(high, lanes // 2, 2))
    packed[1] = jnp.where(left, pltpu.roll(low, lanes // 2, 2), high)

    def d_copy(n, core):
        return pltpu.make_async_remote_copy(
            src_ref=packed.at[core, n], dst_ref=dom_in.at[d],
            send_sem=d_send.at[core, n], recv_sem=d_recv.at[d],
            device_id={"dom": c * group + n, "rep": y * 2 + core}, device_id_type=MESH)

    @pl.loop(0, group)
    def _(m):
        n = lax.rem(m + d + group // 2, group)
        for core in range(2):
            @pl.when((c * group + n != d) | (c != core))
            def _():
                d_copy(n, core).start()

    gi_ref[...] = lax.dot_general(
        agg_ref[...], weight_ref[...], (((1,), (1,)), ((), ())),
        preferred_element_type=f32).astype(gi_ref.dtype)

    @pl.when(c == home)
    def _():
        dom_in[d] = packed[c, d - c * group]

    @pl.loop(0, peers)
    def _(s):
        @pl.when((s != d) | (c != home))
        def _():
            pltpu.make_async_remote_copy(
                src_ref=packed.at[0, 0], dst_ref=dom_in.at[s],
                send_sem=d_send.at[0, 0], recv_sem=d_recv.at[s],
                device_id={"dom": d, "rep": r_pair}, device_id_type=MESH).wait_recv()

    sums_of = [dom_in[s] for s in range(peers)]
    while len(sums_of) > 1:
        sums_of = [a + b for a, b in zip(sums_of[::2], sums_of[1::2])]
    total = sums_of[0]
    out_ref[:out_rows // 2] = total[:, :lanes // 2]
    out_ref[out_rows // 2:] = total[:, lanes // 2:]

    for n in range(ys_n):
        c_copy(n).wait_send()
    for way in range(2):
        s_copy(way).wait_send()
        for part in range(2):
            h_copy(way, part).wait_send()
    @pl.loop(0, group)
    def _(n):
        for core in range(2):
            @pl.when((c * group + n != d) | (c != core))
            def _():
                d_copy(n, core).wait_send()

    @pl.loop(1, peers)
    def _(n):
        a_copy(n, z, x).wait_send()

    @pl.loop(0, zs_n)
    def _(j):
        for way in range(2):
            y_copy(j, way, r).wait_send()
            f_copy(j, way, r).wait_send()
        for which in range(4):
            p_copy(j, which, r).wait_send()


def layer(perm, grad, index, count, edge, feat, weight, scale):
    zs_n, xs_n, ys_n = SIZES
    rows, width = grad.shape
    fin = feat.shape[1]
    reps, doms = 2 * ys_n, zs_n * xs_n
    piece = rows // doms
    slots, side = edge.shape[0], edge.shape[1]
    tall, lanes = fin // 2, width // ys_n
    out_rows = fin // doms
    far = pl.BlockSpec(memory_space=pltpu.HBM)
    vmem = pl.BlockSpec(memory_space=pltpu.VMEM)
    dma = pltpu.SemaphoreType.DMA
    f32, bf16 = jnp.float32, grad.dtype
    args = (perm.reshape(1, rows), grad, index, count, edge, feat, weight)
    args = tuple(a if n == 3 else pltpu.with_memory_space_constraint(a, pltpu.HBM)
                 for n, a in enumerate(args))
    return pl.pallas_call(
        lambda *refs: layer_kernel(zs_n, xs_n, ys_n, scale, *refs),
        out_shape=(jax.ShapeDtypeStruct((rows, fin), bf16),
                   jax.ShapeDtypeStruct((out_rows, lanes // 2), f32)),
        in_specs=[far] * 3 + [pl.BlockSpec(memory_space=pltpu.SMEM)] + [far] * 3,
        out_specs=(vmem, vmem),
        scratch_shapes=[
            pltpu.VMEM((1, rows), jnp.int32),
            pltpu.VMEM(grad.shape, bf16),
            pltpu.VMEM(index.shape, jnp.int32),
            pltpu.VMEM(edge.shape, bf16),
            pltpu.VMEM(feat.shape, bf16),
            pltpu.VMEM(weight.shape, bf16),
            pltpu.VMEM((rows, width), bf16),
            pltpu.VMEM((zs_n, xs_n, reps, piece, width), bf16),
            pltpu.VMEM((256, 256), bf16),
            pltpu.VMEM((8, slots), jnp.int32),
            pltpu.SMEM((8, slots), jnp.int32),
            pltpu.VMEM((side, side), f32),
            pltpu.VMEM((slots + 1, side, side), bf16),
            pltpu.VMEM((rows, rows), bf16),
            pltpu.VMEM((rows, width), bf16),
            pltpu.VMEM((rows, width), f32),
            pltpu.VMEM((rows, width), bf16),
            pltpu.VMEM((tall, width), f32), pltpu.VMEM((tall, width), f32),
            pltpu.VMEM((ys_n, tall, lanes), f32), pltpu.VMEM((ys_n, tall, lanes), f32),
            pltpu.VMEM((2, tall // 2, lanes), f32), pltpu.VMEM((2, tall, lanes), f32),
            pltpu.VMEM((tall, lanes), f32),
            pltpu.VMEM((2, doms // 2, out_rows // 2, lanes), f32),
            pltpu.VMEM((doms, out_rows // 2, lanes), f32),
            dma((6,)), dma, dma, dma((doms,)), dma((doms,)),
            dma((2, zs_n)), dma((2, zs_n)), dma((2, zs_n)), dma((2, zs_n)),
            dma((4, zs_n)), dma((4, zs_n)),
            dma((ys_n,)), dma((ys_n,)), dma((2,)), dma((2,)), dma((2, 2)), dma((2, 2)),
            dma((2, doms // 2)), dma((doms,)),
        ],
        compiler_params=pltpu.CompilerParams(
            collective_id=0, has_side_effects=True, vmem_limit_bytes=46 << 20),
        name="layer",
    )(*args)


def on_device(grad_out, features, weight, edge_blocks, block_index, block_count, node_perm):
    nodes = grad_out.shape[0] * lax.axis_size("dom") * lax.axis_size("rep")
    return layer(node_perm, grad_out, block_index.T, block_count, edge_blocks, features, weight,
                 1.0 / math.sqrt(nodes))


def solution(mesh):
    in_specs = (
        P(("dom", "rep"), None),
        P(("dom", "rep"), None),
        P(),
        P(("dom", "rep"), None, None),
        P(("dom", "rep"), None),
        P(("dom", "rep")),
        P(("dom", "rep")),
    )
    out_specs = (P(("dom", "rep"), None), P("dom", "rep"))
    return jax.shard_map(
        on_device, mesh=mesh, in_specs=in_specs, out_specs=out_specs, check_vma=False
    )
```

```python
import math

import jax
import jax.numpy as jnp
from jax import lax
from jax.experimental import pallas as pl
from jax.experimental.pallas import tpu as pltpu
from jax.sharding import PartitionSpec as P

MESH = pl.DeviceIdType.MESH
SIZES = (8, 4, 4)


def wrap(value, size):
    return lax.rem(value + 2 * size, size)


def make_table(index, live):
    count = index.shape[1]
    here = lax.broadcasted_iota(jnp.int32, (count, count), 0).astype(jnp.float32)
    lane = lax.broadcasted_iota(jnp.int32, (count, count), 1)
    pair = jnp.broadcast_to(index[0:1, :] * 8 + index[1:2, :], (count, count))
    across = jnp.where(lane < live, pair, 4 * count).astype(jnp.float32)
    lane = lane.astype(jnp.float32)
    key = across.T

    def total(mask, value=1.0):
        return jnp.sum(jnp.where(mask, value, 0.0), axis=0, keepdims=True)

    ahead = (across < key) | ((across == key) & (lane < here))
    rank = jnp.sum(jnp.where(ahead, 1.0, 0.0), axis=1, keepdims=True)
    slot = total(rank == lane, here)
    now = total(rank == lane, key)
    before = total(rank == lane - 1.0, key)
    same = jnp.where((now == before) & (lane[0:1] > 0.0), 1.0, 0.0)
    rows = [slot, same]
    for part in range(4):
        wanted = lane + float(part * count)
        found = total(key <= wanted) - 1.0
        rows.append(jnp.where(total(key == wanted) > 0.0, found, float(count)))
    rows.append(jnp.zeros((2, count), jnp.float32))
    return jnp.concatenate(rows, axis=0).astype(jnp.int32)


def layer_kernel(
        zs_n, xs_n, ys_n, scale,
        perm_hbm, grad_hbm, index_hbm, count_ref, edge_hbm, feat_hbm,
        weight_hbm, gi_ref, out_ref,
        perm_ref, grad_ref, index_ref, edge_ref, feat_ref, weight_ref, ordered, raw, unperm,
        table_ref, tab, running, summed, dense, chunk, acc, agg_ref,
        part_other, part_mine, pair_in, sums, far_in, y_in, cols_sum, packed, dom_in,
        load_sem, own_sem, tab_sem, a_send, a_recv, y_send, y_recv, f_send, f_recv, p_send, p_recv,
        c_send, c_recv, s_send, s_recv, h_send, h_recv, d_send, d_recv):
    d = lax.axis_index("dom")
    r = lax.axis_index("rep")
    z, x = d // xs_n, lax.rem(d, xs_n)
    y, c = r // 2, lax.rem(r, 2)
    peers = zs_n * xs_n
    slot_rows = 4
    piece = 2 * ys_n * slot_rows
    side = edge_ref.shape[1]
    r_up = wrap(y + 1, ys_n) * 2 + c
    r_down = wrap(y - 1, ys_n) * 2 + c
    r_far = wrap(y + 2, ys_n) * 2 + c
    r_pair = r + 1 - 2 * c
    r_way = (r_up, r_down)
    group = peers // 2
    home = d // group
    bf16, f32 = jnp.bfloat16, jnp.float32

    def offset(j):
        return ((j + 1) // 2) * (2 * lax.rem(j, 2) - 1)

    loads = [pltpu.make_async_copy(a, b, load_sem.at[n]) for n, (a, b) in enumerate((
        (perm_hbm, perm_ref), (grad_hbm, grad_ref), (index_hbm, index_ref),
        (edge_hbm, edge_ref), (feat_hbm, feat_ref), (weight_hbm, weight_ref)))]
    for load in loads[:3]:
        load.start()

    barrier = pltpu.get_barrier_semaphore()

    @pl.loop(0, peers - 1)
    def _(n):
        to = wrap(d + 1 + lax.rem(n + peers // 2 - 4, peers - 1), peers)
        pl.semaphore_signal(barrier, inc=1, device_id={"dom": to, "rep": r},
                            device_id_type=MESH)

    for other in (*r_way, r_pair):
        pl.semaphore_signal(barrier, inc=1, device_id={"dom": d, "rep": other},
                            device_id_type=MESH)

    @pl.when(c != home)
    def _():
        @pl.loop(0, peers)
        def _(n):
            pl.semaphore_signal(barrier, inc=1,
                                device_id={"dom": wrap(d + n + peers // 2 - 4, peers),
                                           "rep": r_pair},
                                device_id_type=MESH)

    loads[0].wait()
    perm = perm_ref[...]
    target = (perm // grad_ref.shape[0]) * slot_rows + lax.rem(perm, slot_rows)
    tile = 256
    loads[1].wait()
    for load in loads[3:]:
        load.start()

    @pl.loop(0, grad_ref.shape[0] // tile)
    def _(t):
        rows = lax.broadcasted_iota(jnp.int32, (tile, grad_ref.shape[0]), 0) + t * tile
        hot = jnp.where(rows == target, 1.0, 0.0).astype(bf16)
        ordered[pl.ds(pl.multiple_of(t * tile, tile), tile), :] = lax.dot_general(
            hot, grad_ref[...], (((1,), (0,)), ((), ())), preferred_element_type=f32).astype(bf16)

    pl.semaphore_wait(barrier, peers - 1 + 3 + group)

    own = pltpu.make_async_copy(
        ordered.at[pl.ds(pl.multiple_of(d * piece, piece), piece)], raw.at[z, x, r], own_sem)
    own.start()

    def a_copy(n, zs, xs):
        j, i = n // xs_n, lax.rem(n, xs_n)
        to = wrap(z + offset(j), zs_n) * xs_n + wrap(x + i, xs_n)
        return pltpu.make_async_remote_copy(
            src_ref=ordered.at[pl.ds(pl.multiple_of(to * piece, piece), piece)],
            dst_ref=raw.at[zs, xs, r],
            send_sem=a_send.at[n], recv_sem=a_recv.at[n],
            device_id={"dom": to, "rep": r}, device_id_type=MESH)

    @pl.loop(1, peers)
    def _(n):
        a_copy(n, z, x).start()

    loads[2].wait()
    table_ref[...] = make_table(index_ref[...], count_ref[0])
    tab_copy = pltpu.make_async_copy(table_ref, tab, tab_sem)
    tab_copy.start()
    q = lax.broadcasted_iota(jnp.int32, (tile, tile), 0)
    p = lax.broadcasted_iota(jnp.int32, (tile, tile), 1)
    wanted = lax.rem(q // slot_rows, 8) * piece + (q // piece) * slot_rows + lax.rem(q, slot_rows)
    unperm[...] = jnp.where(p == wanted, 1.0, 0.0).astype(bf16)

    def chunk_of(j):
        return wrap(z - offset(j), zs_n)

    def y_copy(j, way, owner):
        part = raw.at[chunk_of(j), :, owner]
        return pltpu.make_async_remote_copy(
            src_ref=part, dst_ref=part, send_sem=y_send.at[way, j], recv_sem=y_recv.at[way, j],
            device_id={"dom": d, "rep": r_way[way]}, device_id_type=MESH)

    half = xs_n // 2

    def f_copy(j, way, owner):
        part = raw.at[chunk_of(j), pl.ds(way * half, half), owner]
        return pltpu.make_async_remote_copy(
            src_ref=part, dst_ref=part, send_sem=f_send.at[way, j], recv_sem=f_recv.at[way, j],
            device_id={"dom": d, "rep": r_way[way]}, device_id_type=MESH)

    def p_copy(j, which, owner):
        part = raw.at[chunk_of(j), :, owner]
        return pltpu.make_async_remote_copy(
            src_ref=part, dst_ref=part, send_sem=p_send.at[which, j],
            recv_sem=p_recv.at[which, j],
            device_id={"dom": d, "rep": r_pair}, device_id_type=MESH)

    quarter = edge_ref.shape[0] // 4

    def sum_pairs(part):
        @pl.loop(0, quarter)
        def _(n):
            at = part * quarter + n
            slot = jnp.clip(tab[0, at], 0, edge_ref.shape[0] - 1)
            total = jnp.where(tab[1, at] > 0, running[...], 0.0) + edge_ref[slot].astype(f32)
            running[...] = total
            summed[at] = total.T.astype(bf16)

    def send_own(j):
        @pl.loop(0, xs_n)
        def _(i):
            @pl.when(j * xs_n + i > 0)
            def _():
                a_copy(j * xs_n + i, chunk_of(j), wrap(x - i, xs_n)).wait_recv()

        y_copy(j, 0, r).start()
        y_copy(j, 1, r).start()
        p_copy(j, 0, r).start()

    own.wait()
    send_own(0)
    loads[3].wait()
    tab_copy.wait()
    running[...] = jnp.zeros_like(running)
    summed[edge_ref.shape[0]] = jnp.zeros((side, side), bf16)
    sum_pairs(0)
    acc[...] = jnp.zeros_like(acc)

    @pl.loop(0, zs_n + 3)
    def _(step):
        @pl.when(step + 1 < zs_n)
        def _():
            send_own(step + 1)

        @pl.when((step >= 1) & (step < zs_n + 1))
        def _():
            j = step - 1
            y_copy(j, 0, r_down).wait_recv()
            f_copy(j, 0, r_down).start()
            p_copy(j, 1, r_down).start()
            y_copy(j, 1, r_up).wait_recv()
            f_copy(j, 1, r_up).start()
            p_copy(j, 2, r_up).start()

        @pl.when(step < 3)
        def _():
            sum_pairs(step + 1)

        @pl.when(step >= 3)
        def _():
            j = step - 3
            zs = chunk_of(j)
            for t in range(8):
                for col in range(8):
                    pair = t * 64 + zs * 8 + col
                    place = tab[2 + pair // side, lax.rem(pair, side)]
                    dense[col * side:(col + 1) * side, t * side:(t + 1) * side] = summed[
                        jnp.clip(place, 0, edge_ref.shape[0])]
            flip = 1 - 2 * c
            p_copy(j, 0, r + flip).wait_recv()
            p_copy(j, 1, r_down + flip).wait_recv()
            p_copy(j, 2, r_up + flip).wait_recv()
            p_copy(j, 3, r_far + flip).wait_recv()
            for xs in range(xs_n):
                rows = raw[zs, xs].reshape(tile, acc.shape[1])
                placed = lax.dot_general(
                    unperm[...], rows, (((1,), (0,)), ((), ())),
                    preferred_element_type=f32).astype(bf16)
                for t in range(2 * ys_n):
                    chunk[t * side + xs * piece:t * side + (xs + 1) * piece, :] = placed[
                        t * piece:(t + 1) * piece, :]
            acc[...] += lax.dot_general(
                dense[...], chunk[...], (((1,), (0,)), ((), ())), preferred_element_type=f32)

        @pl.when((step >= 2) & (step < zs_n + 2))
        def _():
            j = step - 2
            f_copy(j, 0, r_far).wait_recv()
            f_copy(j, 1, r_far).wait_recv()
            p_copy(j, 3, r_far).start()

    agg_ref[...] = acc[...].astype(bf16)
    for load in loads[4:]:
        load.wait()
    out_rows = out_ref.shape[0]
    tall, lanes = cols_sum.shape
    mid = tall // 2

    def partial(half):
        cols = feat_ref[:, pl.ds(pl.multiple_of(half * tall, tall), tall)]
        return lax.dot_general(
            cols, agg_ref[...], (((0,), (0,)), ((), ())),
            preferred_element_type=jnp.float32) * scale

    part_other[...] = partial(1 - c)

    def wide(n):
        return pl.ds(pl.multiple_of(wrap(y + n, ys_n) * lanes, lanes), lanes)

    def c_copy(n):
        return pltpu.make_async_remote_copy(
            src_ref=part_other.at[:, wide(n)], dst_ref=pair_in.at[n],
            send_sem=c_send.at[n], recv_sem=c_recv.at[n],
            device_id={"dom": d, "rep": r_pair}, device_id_type=MESH)

    def s_copy(way):
        return pltpu.make_async_remote_copy(
            src_ref=sums.at[2, pl.ds(way * mid, mid)], dst_ref=far_in.at[way],
            send_sem=s_send.at[way], recv_sem=s_recv.at[way],
            device_id={"dom": d, "rep": r_way[way]}, device_id_type=MESH)

    def h_copy(way, part):
        place = pl.ds(part * mid, mid)
        return pltpu.make_async_remote_copy(
            src_ref=sums.at[1 + 2 * way, place], dst_ref=y_in.at[way, place],
            send_sem=h_send.at[way, part], recv_sem=h_recv.at[way, part],
            device_id={"dom": d, "rep": r_way[way]}, device_id_type=MESH)

    def add_pair(n):
        c_copy(n).wait_recv()
        sums[n] = part_mine[:, wide(n)] + pair_in[n]

    for n in (2, 1, 3, 0):
        c_copy(n).start()
    part_mine[...] = partial(c)
    add_pair(2)
    for way in range(2):
        s_copy(way).start()
    for way in range(2):
        add_pair(1 + 2 * way)
        h_copy(way, 1 - way).start()
    add_pair(0)
    for way in range(2):
        s_copy(way).wait_recv()
        sums[1 + 2 * way, way * mid:(way + 1) * mid] += far_in[way]
        h_copy(way, way).start()
    for way in range(2):
        h_copy(way, 1 - way).wait_recv()
    for way in range(2):
        h_copy(way, way).wait_recv()
    cols_sum[...] = sums[0] + (y_in[0] + y_in[1])
    both = cols_sum[...].reshape(group, out_rows, lanes)
    low, high = both[:, :out_rows // 2], both[:, out_rows // 2:]
    left = lax.broadcasted_iota(jnp.int32, low.shape, 2) < lanes // 2
    packed[0] = jnp.where(left, low, pltpu.roll(high, lanes // 2, 2))
    packed[1] = jnp.where(left, pltpu.roll(low, lanes // 2, 2), high)

    def d_copy(n, core):
        return pltpu.make_async_remote_copy(
            src_ref=packed.at[core, n], dst_ref=dom_in.at[d],
            send_sem=d_send.at[core, n], recv_sem=d_recv.at[d],
            device_id={"dom": c * group + n, "rep": y * 2 + core}, device_id_type=MESH)

    @pl.loop(0, group)
    def _(m):
        n = lax.rem(m + d + group // 2, group)
        for core in range(2):
            @pl.when((c * group + n != d) | (c != core))
            def _():
                d_copy(n, core).start()

    gi_ref[...] = lax.dot_general(
        agg_ref[...], weight_ref[...], (((1,), (1,)), ((), ())),
        preferred_element_type=f32).astype(gi_ref.dtype)

    @pl.when(c == home)
    def _():
        dom_in[d] = packed[c, d - c * group]

    @pl.loop(0, peers)
    def _(s):
        @pl.when((s != d) | (c != home))
        def _():
            pltpu.make_async_remote_copy(
                src_ref=packed.at[0, 0], dst_ref=dom_in.at[s],
                send_sem=d_send.at[0, 0], recv_sem=d_recv.at[s],
                device_id={"dom": d, "rep": r_pair}, device_id_type=MESH).wait_recv()

    sums_of = [dom_in[s] for s in range(peers)]
    while len(sums_of) > 1:
        sums_of = [a + b for a, b in zip(sums_of[::2], sums_of[1::2])]
    total = sums_of[0]
    out_ref[:out_rows // 2] = total[:, :lanes // 2]
    out_ref[out_rows // 2:] = total[:, lanes // 2:]

    for n in range(ys_n):
        c_copy(n).wait_send()
    for way in range(2):
        s_copy(way).wait_send()
        for part in range(2):
            h_copy(way, part).wait_send()
    @pl.loop(0, group)
    def _(n):
        for core in range(2):
            @pl.when((c * group + n != d) | (c != core))
            def _():
                d_copy(n, core).wait_send()

    @pl.loop(1, peers)
    def _(n):
        a_copy(n, z, x).wait_send()

    @pl.loop(0, zs_n)
    def _(j):
        for way in range(2):
            y_copy(j, way, r).wait_send()
            f_copy(j, way, r).wait_send()
        for which in range(4):
            p_copy(j, which, r).wait_send()


def layer(perm, grad, index, count, edge, feat, weight, scale):
    zs_n, xs_n, ys_n = SIZES
    rows, width = grad.shape
    fin = feat.shape[1]
    reps, doms = 2 * ys_n, zs_n * xs_n
    piece = rows // doms
    slots, side = edge.shape[0], edge.shape[1]
    tall, lanes = fin // 2, width // ys_n
    out_rows = fin // doms
    far = pl.BlockSpec(memory_space=pltpu.HBM)
    vmem = pl.BlockSpec(memory_space=pltpu.VMEM)
    dma = pltpu.SemaphoreType.DMA
    f32, bf16 = jnp.float32, grad.dtype
    args = (perm.reshape(1, rows), grad, index, count, edge, feat, weight)
    args = tuple(a if n == 3 else pltpu.with_memory_space_constraint(a, pltpu.HBM)
                 for n, a in enumerate(args))
    return pl.pallas_call(
        lambda *refs: layer_kernel(zs_n, xs_n, ys_n, scale, *refs),
        out_shape=(jax.ShapeDtypeStruct((rows, fin), bf16),
                   jax.ShapeDtypeStruct((out_rows, lanes // 2), f32)),
        in_specs=[far] * 3 + [pl.BlockSpec(memory_space=pltpu.SMEM)] + [far] * 3,
        out_specs=(vmem, vmem),
        scratch_shapes=[
            pltpu.VMEM((1, rows), jnp.int32),
            pltpu.VMEM(grad.shape, bf16),
            pltpu.VMEM(index.shape, jnp.int32),
            pltpu.VMEM(edge.shape, bf16),
            pltpu.VMEM(feat.shape, bf16),
            pltpu.VMEM(weight.shape, bf16),
            pltpu.VMEM((rows, width), bf16),
            pltpu.VMEM((zs_n, xs_n, reps, piece, width), bf16),
            pltpu.VMEM((256, 256), bf16),
            pltpu.VMEM((8, slots), jnp.int32),
            pltpu.SMEM((8, slots), jnp.int32),
            pltpu.VMEM((side, side), f32),
            pltpu.VMEM((slots + 1, side, side), bf16),
            pltpu.VMEM((rows, rows), bf16),
            pltpu.VMEM((rows, width), bf16),
            pltpu.VMEM((rows, width), f32),
            pltpu.VMEM((rows, width), bf16),
            pltpu.VMEM((tall, width), f32), pltpu.VMEM((tall, width), f32),
            pltpu.VMEM((ys_n, tall, lanes), f32), pltpu.VMEM((ys_n, tall, lanes), f32),
            pltpu.VMEM((2, tall // 2, lanes), f32), pltpu.VMEM((2, tall, lanes), f32),
            pltpu.VMEM((tall, lanes), f32),
            pltpu.VMEM((2, doms // 2, out_rows // 2, lanes), f32),
            pltpu.VMEM((doms, out_rows // 2, lanes), f32),
            dma((6,)), dma, dma, dma((doms,)), dma((doms,)),
            dma((2, zs_n)), dma((2, zs_n)), dma((2, zs_n)), dma((2, zs_n)),
            dma((4, zs_n)), dma((4, zs_n)),
            dma((ys_n,)), dma((ys_n,)), dma((2,)), dma((2,)), dma((2, 2)), dma((2, 2)),
            dma((2, doms // 2)), dma((doms,)),
        ],
        compiler_params=pltpu.CompilerParams(
            collective_id=0, has_side_effects=True, vmem_limit_bytes=46 << 20),
        name="layer",
    )(*args)


def store_kernel(gi_ref, sum_ref, gi_hbm, sum_hbm, sems):
    copies = [pltpu.make_async_copy(gi_ref, gi_hbm, sems.at[0]),
              pltpu.make_async_copy(sum_ref, sum_hbm, sems.at[1])]
    for copy in copies:
        copy.start()
    for copy in copies:
        copy.wait()


def store(*values):
    vmem = pl.BlockSpec(memory_space=pltpu.VMEM)
    far = pl.BlockSpec(memory_space=pltpu.HBM)
    return pl.pallas_call(
        store_kernel,
        out_shape=tuple(jax.ShapeDtypeStruct(a.shape, a.dtype) for a in values),
        in_specs=[vmem, vmem],
        out_specs=(far, far),
        scratch_shapes=[pltpu.SemaphoreType.DMA((2,))],
        compiler_params=pltpu.CompilerParams(vmem_limit_bytes=4 << 20),
        name="store",
    )(*values)


def on_device(grad_out, features, weight, edge_blocks, block_index, block_count, node_perm):
    nodes = grad_out.shape[0] * lax.axis_size("dom") * lax.axis_size("rep")
    return store(*layer(
        node_perm, grad_out, block_index.T, block_count, edge_blocks, features, weight,
        1.0 / math.sqrt(nodes)))


def solution(mesh):
    in_specs = (
        P(("dom", "rep"), None),
        P(("dom", "rep"), None),
        P(),
        P(("dom", "rep"), None, None),
        P(("dom", "rep"), None),
        P(("dom", "rep")),
        P(("dom", "rep")),
    )
    out_specs = (P(("dom", "rep"), None), P("dom", "rep"))
    return jax.shard_map(
        on_device, mesh=mesh, in_specs=in_specs, out_specs=out_specs, check_vma=False
    )
```

```python
import math

import jax
import jax.numpy as jnp
from jax import lax
from jax.experimental import pallas as pl
from jax.experimental.pallas import tpu as pltpu
from jax.sharding import PartitionSpec as P

MESH = pl.DeviceIdType.MESH
SIZES = (8, 4, 4)


def wrap(value, size):
    return lax.rem(value + 2 * size, size)


def make_table(index, live):
    count = index.shape[1]
    here = lax.broadcasted_iota(jnp.int32, (count, count), 0).astype(jnp.float32)
    lane = lax.broadcasted_iota(jnp.int32, (count, count), 1)
    pair = jnp.broadcast_to(index[0:1, :] * 8 + index[1:2, :], (count, count))
    across = jnp.where(lane < live, pair, 4 * count).astype(jnp.float32)
    lane = lane.astype(jnp.float32)
    key = across.T

    def total(mask, value=1.0):
        return jnp.sum(jnp.where(mask, value, 0.0), axis=0, keepdims=True)

    ahead = (across < key) | ((across == key) & (lane < here))
    rank = jnp.sum(jnp.where(ahead, 1.0, 0.0), axis=1, keepdims=True)
    slot = total(rank == lane, here)
    now = total(rank == lane, key)
    before = total(rank == lane - 1.0, key)
    same = jnp.where((now == before) & (lane[0:1] > 0.0), 1.0, 0.0)
    rows = [slot, same]
    for part in range(4):
        wanted = lane + float(part * count)
        found = total(key <= wanted) - 1.0
        rows.append(jnp.where(total(key == wanted) > 0.0, found, float(count)))
    rows.append(jnp.zeros((2, count), jnp.float32))
    return jnp.concatenate(rows, axis=0).astype(jnp.int32)


def layer_kernel(
        zs_n, xs_n, ys_n, scale,
        perm_hbm, grad_hbm, index_hbm, count_ref, edge_hbm, feat_hbm,
        weight_hbm, gi_ref, out_ref,
        perm_ref, grad_ref, index_ref, edge_ref, feat_ref, weight_ref, feat_cols, ordered, raw, unperm,
        table_ref, tab, running, summed, dense, chunk, acc, agg_ref,
        part_other, part_mine, pair_in, sums, far_in, y_in, cols_sum, packed, dom_in,
        load_sem, own_sem, tab_sem, a_send, a_recv, y_send, y_recv, f_send, f_recv, p_send, p_recv,
        c_send, c_recv, s_send, s_recv, h_send, h_recv, d_send, d_recv):
    d = lax.axis_index("dom")
    r = lax.axis_index("rep")
    z, x = d // xs_n, lax.rem(d, xs_n)
    y, c = r // 2, lax.rem(r, 2)
    peers = zs_n * xs_n
    slot_rows = 4
    piece = 2 * ys_n * slot_rows
    side = edge_ref.shape[1]
    r_up = wrap(y + 1, ys_n) * 2 + c
    r_down = wrap(y - 1, ys_n) * 2 + c
    r_far = wrap(y + 2, ys_n) * 2 + c
    r_pair = r + 1 - 2 * c
    r_way = (r_up, r_down)
    group = peers // 2
    home = d // group
    bf16, f32 = jnp.bfloat16, jnp.float32

    def offset(j):
        return ((j + 1) // 2) * (2 * lax.rem(j, 2) - 1)

    loads = [pltpu.make_async_copy(a, b, load_sem.at[n]) for n, (a, b) in enumerate((
        (perm_hbm, perm_ref), (grad_hbm, grad_ref), (index_hbm, index_ref),
        (edge_hbm, edge_ref), (feat_hbm, feat_ref), (weight_hbm, weight_ref)))]
    for load in loads[:3]:
        load.start()

    barrier = pltpu.get_barrier_semaphore()

    @pl.loop(0, peers - 1)
    def _(n):
        to = wrap(d + 1 + lax.rem(n + peers // 2 - 4, peers - 1), peers)
        pl.semaphore_signal(barrier, inc=1, device_id={"dom": to, "rep": r},
                            device_id_type=MESH)

    for other in (*r_way, r_pair):
        pl.semaphore_signal(barrier, inc=1, device_id={"dom": d, "rep": other},
                            device_id_type=MESH)

    @pl.when(c != home)
    def _():
        @pl.loop(0, peers)
        def _(n):
            pl.semaphore_signal(barrier, inc=1,
                                device_id={"dom": wrap(d + n + peers // 2 - 4, peers),
                                           "rep": r_pair},
                                device_id_type=MESH)

    loads[0].wait()
    perm = perm_ref[...]
    target = (perm // grad_ref.shape[0]) * slot_rows + lax.rem(perm, slot_rows)
    tile = 256
    loads[1].wait()
    for load in loads[3:]:
        load.start()

    @pl.loop(0, grad_ref.shape[0] // tile)
    def _(t):
        rows = lax.broadcasted_iota(jnp.int32, (tile, grad_ref.shape[0]), 0) + t * tile
        hot = jnp.where(rows == target, 1.0, 0.0).astype(bf16)
        ordered[pl.ds(pl.multiple_of(t * tile, tile), tile), :] = lax.dot_general(
            hot, grad_ref[...], (((1,), (0,)), ((), ())), preferred_element_type=f32).astype(bf16)

    pl.semaphore_wait(barrier, peers - 1 + 3 + group)

    own = pltpu.make_async_copy(
        ordered.at[pl.ds(pl.multiple_of(d * piece, piece), piece)], raw.at[z, x, r], own_sem)
    own.start()

    def a_copy(n, zs, xs):
        j, i = n // xs_n, lax.rem(n, xs_n)
        to = wrap(z + offset(j), zs_n) * xs_n + wrap(x + i, xs_n)
        return pltpu.make_async_remote_copy(
            src_ref=ordered.at[pl.ds(pl.multiple_of(to * piece, piece), piece)],
            dst_ref=raw.at[zs, xs, r],
            send_sem=a_send.at[n], recv_sem=a_recv.at[n],
            device_id={"dom": to, "rep": r}, device_id_type=MESH)

    @pl.loop(1, peers)
    def _(n):
        a_copy(n, z, x).start()

    loads[2].wait()
    table_ref[...] = make_table(index_ref[...], count_ref[0])
    tab_copy = pltpu.make_async_copy(table_ref, tab, tab_sem)
    tab_copy.start()
    q = lax.broadcasted_iota(jnp.int32, (tile, tile), 0)
    p = lax.broadcasted_iota(jnp.int32, (tile, tile), 1)
    wanted = lax.rem(q // slot_rows, 8) * piece + (q // piece) * slot_rows + lax.rem(q, slot_rows)
    unperm[...] = jnp.where(p == wanted, 1.0, 0.0).astype(bf16)

    def chunk_of(j):
        return wrap(z - offset(j), zs_n)

    def y_copy(j, way, owner):
        part = raw.at[chunk_of(j), :, owner]
        return pltpu.make_async_remote_copy(
            src_ref=part, dst_ref=part, send_sem=y_send.at[way, j], recv_sem=y_recv.at[way, j],
            device_id={"dom": d, "rep": r_way[way]}, device_id_type=MESH)

    half = xs_n // 2

    def f_copy(j, way, owner):
        part = raw.at[chunk_of(j), pl.ds(way * half, half), owner]
        return pltpu.make_async_remote_copy(
            src_ref=part, dst_ref=part, send_sem=f_send.at[way, j], recv_sem=f_recv.at[way, j],
            device_id={"dom": d, "rep": r_way[way]}, device_id_type=MESH)

    def p_copy(j, which, owner):
        part = raw.at[chunk_of(j), :, owner]
        return pltpu.make_async_remote_copy(
            src_ref=part, dst_ref=part, send_sem=p_send.at[which, j],
            recv_sem=p_recv.at[which, j],
            device_id={"dom": d, "rep": r_pair}, device_id_type=MESH)

    quarter = edge_ref.shape[0] // 4

    def sum_pairs(part):
        @pl.loop(0, quarter)
        def _(n):
            at = part * quarter + n
            slot = jnp.clip(tab[0, at], 0, edge_ref.shape[0] - 1)
            total = jnp.where(tab[1, at] > 0, running[...], 0.0) + edge_ref[slot].astype(f32)
            running[...] = total
            summed[at] = total.T.astype(bf16)

    def send_own(j):
        @pl.loop(0, xs_n)
        def _(i):
            @pl.when(j * xs_n + i > 0)
            def _():
                a_copy(j * xs_n + i, chunk_of(j), wrap(x - i, xs_n)).wait_recv()

        y_copy(j, 0, r).start()
        y_copy(j, 1, r).start()
        p_copy(j, 0, r).start()

    own.wait()
    send_own(0)
    loads[3].wait()
    tab_copy.wait()
    running[...] = jnp.zeros_like(running)
    summed[edge_ref.shape[0]] = jnp.zeros((side, side), bf16)
    sum_pairs(0)
    acc[...] = jnp.zeros_like(acc)

    @pl.loop(0, zs_n + 3)
    def _(step):
        @pl.when(step + 1 < zs_n)
        def _():
            send_own(step + 1)

        @pl.when((step >= 1) & (step < zs_n + 1))
        def _():
            j = step - 1
            y_copy(j, 0, r_down).wait_recv()
            f_copy(j, 0, r_down).start()
            p_copy(j, 1, r_down).start()
            y_copy(j, 1, r_up).wait_recv()
            f_copy(j, 1, r_up).start()
            p_copy(j, 2, r_up).start()

        @pl.when(step < 3)
        def _():
            sum_pairs(step + 1)

        @pl.when(step == 1)
        def _():
            loads[4].wait()
            feat_cols[...] = feat_ref[...].T

        @pl.when(step >= 3)
        def _():
            j = step - 3
            zs = chunk_of(j)
            for t in range(8):
                for col in range(8):
                    pair = t * 64 + zs * 8 + col
                    place = tab[2 + pair // side, lax.rem(pair, side)]
                    dense[col * side:(col + 1) * side, t * side:(t + 1) * side] = summed[
                        jnp.clip(place, 0, edge_ref.shape[0])]
            flip = 1 - 2 * c
            p_copy(j, 0, r + flip).wait_recv()
            p_copy(j, 1, r_down + flip).wait_recv()
            p_copy(j, 2, r_up + flip).wait_recv()
            p_copy(j, 3, r_far + flip).wait_recv()
            for xs in range(xs_n):
                rows = raw[zs, xs].reshape(tile, acc.shape[1])
                placed = lax.dot_general(
                    unperm[...], rows, (((1,), (0,)), ((), ())),
                    preferred_element_type=f32).astype(bf16)
                for t in range(2 * ys_n):
                    chunk[t * side + xs * piece:t * side + (xs + 1) * piece, :] = placed[
                        t * piece:(t + 1) * piece, :]
            acc[...] += lax.dot_general(
                dense[...], chunk[...], (((1,), (0,)), ((), ())), preferred_element_type=f32)

        @pl.when((step >= 2) & (step < zs_n + 2))
        def _():
            j = step - 2
            f_copy(j, 0, r_far).wait_recv()
            f_copy(j, 1, r_far).wait_recv()
            p_copy(j, 3, r_far).start()

    agg_ref[...] = acc[...].astype(bf16)
    loads[5].wait()
    out_rows = out_ref.shape[0]
    tall, lanes = cols_sum.shape
    mid = tall // 2

    def partial(half):
        cols = feat_cols[pl.ds(pl.multiple_of(half * tall, tall), tall), :]
        return lax.dot_general(
            cols, agg_ref[...], (((1,), (0,)), ((), ())),
            preferred_element_type=jnp.float32) * scale

    part_other[...] = partial(1 - c)

    def wide(n):
        return pl.ds(pl.multiple_of(wrap(y + n, ys_n) * lanes, lanes), lanes)

    def c_copy(n):
        return pltpu.make_async_remote_copy(
            src_ref=part_other.at[:, wide(n)], dst_ref=pair_in.at[n],
            send_sem=c_send.at[n], recv_sem=c_recv.at[n],
            device_id={"dom": d, "rep": r_pair}, device_id_type=MESH)

    def s_copy(way):
        return pltpu.make_async_remote_copy(
            src_ref=sums.at[2, pl.ds(way * mid, mid)], dst_ref=far_in.at[way],
            send_sem=s_send.at[way], recv_sem=s_recv.at[way],
            device_id={"dom": d, "rep": r_way[way]}, device_id_type=MESH)

    def h_copy(way, part):
        place = pl.ds(part * mid, mid)
        return pltpu.make_async_remote_copy(
            src_ref=sums.at[1 + 2 * way, place], dst_ref=y_in.at[way, place],
            send_sem=h_send.at[way, part], recv_sem=h_recv.at[way, part],
            device_id={"dom": d, "rep": r_way[way]}, device_id_type=MESH)

    def add_pair(n):
        c_copy(n).wait_recv()
        sums[n] = part_mine[:, wide(n)] + pair_in[n]

    for n in (2, 1, 3, 0):
        c_copy(n).start()
    part_mine[...] = partial(c)
    add_pair(2)
    for way in range(2):
        s_copy(way).start()
    for way in range(2):
        add_pair(1 + 2 * way)
        h_copy(way, 1 - way).start()
    add_pair(0)
    for way in range(2):
        s_copy(way).wait_recv()
        sums[1 + 2 * way, way * mid:(way + 1) * mid] += far_in[way]
        h_copy(way, way).start()
    for way in range(2):
        h_copy(way, 1 - way).wait_recv()
    for way in range(2):
        h_copy(way, way).wait_recv()
    cols_sum[...] = sums[0] + (y_in[0] + y_in[1])
    both = cols_sum[...].reshape(group, out_rows, lanes)
    low, high = both[:, :out_rows // 2], both[:, out_rows // 2:]
    left = lax.broadcasted_iota(jnp.int32, low.shape, 2) < lanes // 2
    packed[0] = jnp.where(left, low, pltpu.roll(high, lanes // 2, 2))
    packed[1] = jnp.where(left, pltpu.roll(low, lanes // 2, 2), high)

    def d_copy(n, core):
        return pltpu.make_async_remote_copy(
            src_ref=packed.at[core, n], dst_ref=dom_in.at[d],
            send_sem=d_send.at[core, n], recv_sem=d_recv.at[d],
            device_id={"dom": c * group + n, "rep": y * 2 + core}, device_id_type=MESH)

    @pl.loop(0, group)
    def _(m):
        n = lax.rem(m + d + group // 2, group)
        for core in range(2):
            @pl.when((c * group + n != d) | (c != core))
            def _():
                d_copy(n, core).start()

    gi_ref[...] = lax.dot_general(
        agg_ref[...], weight_ref[...], (((1,), (1,)), ((), ())),
        preferred_element_type=f32).astype(gi_ref.dtype)

    for n in range(ys_n):
        c_copy(n).wait_send()
    for way in range(2):
        s_copy(way).wait_send()
        for part in range(2):
            h_copy(way, part).wait_send()
    @pl.loop(0, group)
    def _(n):
        for core in range(2):
            @pl.when((c * group + n != d) | (c != core))
            def _():
                d_copy(n, core).wait_send()

    @pl.loop(1, peers)
    def _(n):
        a_copy(n, z, x).wait_send()

    @pl.loop(0, zs_n)
    def _(j):
        for way in range(2):
            y_copy(j, way, r).wait_send()
            f_copy(j, way, r).wait_send()
        for which in range(4):
            p_copy(j, which, r).wait_send()

    @pl.when(c == home)
    def _():
        dom_in[d] = packed[c, d - c * group]

    @pl.loop(0, peers)
    def _(s):
        @pl.when((s != d) | (c != home))
        def _():
            pltpu.make_async_remote_copy(
                src_ref=packed.at[0, 0], dst_ref=dom_in.at[s],
                send_sem=d_send.at[0, 0], recv_sem=d_recv.at[s],
                device_id={"dom": d, "rep": r_pair}, device_id_type=MESH).wait_recv()

    sums_of = [dom_in[s] for s in range(peers)]
    while len(sums_of) > 1:
        sums_of = [a + b for a, b in zip(sums_of[::2], sums_of[1::2])]
    total = sums_of[0]
    out_ref[:out_rows // 2] = total[:, :lanes // 2]
    out_ref[out_rows // 2:] = total[:, lanes // 2:]


def layer(perm, grad, index, count, edge, feat, weight, scale):
    zs_n, xs_n, ys_n = SIZES
    rows, width = grad.shape
    fin = feat.shape[1]
    reps, doms = 2 * ys_n, zs_n * xs_n
    piece = rows // doms
    slots, side = edge.shape[0], edge.shape[1]
    tall, lanes = fin // 2, width // ys_n
    out_rows = fin // doms
    far = pl.BlockSpec(memory_space=pltpu.HBM)
    vmem = pl.BlockSpec(memory_space=pltpu.VMEM)
    dma = pltpu.SemaphoreType.DMA
    f32, bf16 = jnp.float32, grad.dtype
    args = (perm.reshape(1, rows), grad, index, count, edge, feat, weight)
    args = tuple(a if n == 3 else pltpu.with_memory_space_constraint(a, pltpu.HBM)
                 for n, a in enumerate(args))
    return pl.pallas_call(
        lambda *refs: layer_kernel(zs_n, xs_n, ys_n, scale, *refs),
        out_shape=(jax.ShapeDtypeStruct((rows, fin), bf16),
                   jax.ShapeDtypeStruct((out_rows, lanes // 2), f32)),
        in_specs=[far] * 3 + [pl.BlockSpec(memory_space=pltpu.SMEM)] + [far] * 3,
        out_specs=(vmem, vmem),
        scratch_shapes=[
            pltpu.VMEM((1, rows), jnp.int32),
            pltpu.VMEM(grad.shape, bf16),
            pltpu.VMEM(index.shape, jnp.int32),
            pltpu.VMEM(edge.shape, bf16),
            pltpu.VMEM(feat.shape, bf16),
            pltpu.VMEM(weight.shape, bf16),
            pltpu.VMEM(feat.shape[::-1], bf16),
            pltpu.VMEM((rows, width), bf16),
            pltpu.VMEM((zs_n, xs_n, reps, piece, width), bf16),
            pltpu.VMEM((256, 256), bf16),
            pltpu.VMEM((8, slots), jnp.int32),
            pltpu.SMEM((8, slots), jnp.int32),
            pltpu.VMEM((side, side), f32),
            pltpu.VMEM((slots + 1, side, side), bf16),
            pltpu.VMEM((rows, rows), bf16),
            pltpu.VMEM((rows, width), bf16),
            pltpu.VMEM((rows, width), f32),
            pltpu.VMEM((rows, width), bf16),
            pltpu.VMEM((tall, width), f32), pltpu.VMEM((tall, width), f32),
            pltpu.VMEM((ys_n, tall, lanes), f32), pltpu.VMEM((ys_n, tall, lanes), f32),
            pltpu.VMEM((2, tall // 2, lanes), f32), pltpu.VMEM((2, tall, lanes), f32),
            pltpu.VMEM((tall, lanes), f32),
            pltpu.VMEM((2, doms // 2, out_rows // 2, lanes), f32),
            pltpu.VMEM((doms, out_rows // 2, lanes), f32),
            dma((6,)), dma, dma, dma((doms,)), dma((doms,)),
            dma((2, zs_n)), dma((2, zs_n)), dma((2, zs_n)), dma((2, zs_n)),
            dma((4, zs_n)), dma((4, zs_n)),
            dma((ys_n,)), dma((ys_n,)), dma((2,)), dma((2,)), dma((2, 2)), dma((2, 2)),
            dma((2, doms // 2)), dma((doms,)),
        ],
        compiler_params=pltpu.CompilerParams(
            collective_id=0, has_side_effects=True, vmem_limit_bytes=46 << 20),
        name="layer",
    )(*args)


def store_kernel(gi_ref, sum_ref, gi_hbm, sum_hbm, sems):
    copies = [pltpu.make_async_copy(gi_ref, gi_hbm, sems.at[0]),
              pltpu.make_async_copy(sum_ref, sum_hbm, sems.at[1])]
    for copy in copies:
        copy.start()
    for copy in copies:
        copy.wait()


def store(*values):
    vmem = pl.BlockSpec(memory_space=pltpu.VMEM)
    far = pl.BlockSpec(memory_space=pltpu.HBM)
    return pl.pallas_call(
        store_kernel,
        out_shape=tuple(jax.ShapeDtypeStruct(a.shape, a.dtype) for a in values),
        in_specs=[vmem, vmem],
        out_specs=(far, far),
        scratch_shapes=[pltpu.SemaphoreType.DMA((2,))],
        compiler_params=pltpu.CompilerParams(vmem_limit_bytes=4 << 20),
        name="store",
    )(*values)


def on_device(grad_out, features, weight, edge_blocks, block_index, block_count, node_perm):
    nodes = grad_out.shape[0] * lax.axis_size("dom") * lax.axis_size("rep")
    return store(*layer(
        node_perm, grad_out, block_index.T, block_count, edge_blocks, features, weight,
        1.0 / math.sqrt(nodes)))


def solution(mesh):
    in_specs = (
        P(("dom", "rep"), None),
        P(("dom", "rep"), None),
        P(),
        P(("dom", "rep"), None, None),
        P(("dom", "rep"), None),
        P(("dom", "rep")),
        P(("dom", "rep")),
    )
    out_specs = (P(("dom", "rep"), None), P("dom", "rep"))
    return jax.shard_map(
        on_device, mesh=mesh, in_specs=in_specs, out_specs=out_specs, check_vma=False
    )
```
